512 devices in a mesh: rel: 16 (over z, core), dev: 32 (over y, x).
Axes of the slice: x: 4, y: 8, z: 8, core: 2. Of those that a mesh axis runs over, the one named last changes fastest.
Arguments:
- src_feat: bfloat16 [16, 8192, 1024], P('rel', 'dev'), may hold values from -6 to 6
- rel_w_in: bfloat16 [16, 1024, 1024], P('rel', 'dev'), may hold values from -0.1875 to 0.1875
- rel_w_out: bfloat16 [16, 1024, 1024], P('rel', 'dev'), may hold values from -0.1875 to 0.1875
- tile_source: int32 [16, 128], P('rel'), may hold values from 0 to 63
- tile_edges: int32 [16, 128, 128], P('rel'), may hold values from 0 to 16383
- tile_count: int32 [16, 128], P('rel'), may hold values from 0 to 128, as said below
- target_feat: bfloat16 [4096, 1024], P(('dev', 'rel')), may hold values from -6 to 6
- norm_gain: float32 [1024], replicated, may hold values from 0.5 to 2
- tgt_w_in: bfloat16 [1024, 2048], P(None, 'rel'), may hold values from -0.1875 to 0.1875
- tgt_w_out: bfloat16 [2048, 1024], P('rel'), may hold values from -0.125 to 0.125
- out_grad: bfloat16 [4096, 1024], P(('dev', 'rel')), may hold values from -6 to 6
Outputs:
- updated: bfloat16 [4096, 1024], P(('dev', 'rel'))
- src_grad: bfloat16 [16, 8192, 1024], P('rel', 'dev')
The draws below stay inside these ranges and needn't reach their ends.
Inputs may be any that keep to these rules, and one draw needn't show every extreme that they name: Tile k of a relation joins target rows 128 * (k // 4) onward with source rows 128 * tile_source onward. `tile_edges`: each entry is t * 128 + s for an edge from in-tile source offset s to in-tile target offset t; entries past a tile's count are ignored; the same edge may stand several times. The first tile_count entries of a tile's row of tile_edges are its edges; 0 marks an empty tile; in every relation some tile holds 128 edges.
All inputs are finite; a program needn't handle non-finite values.
Results may differ from the reference program's by a relative error of at most 0.013.
Values may be sent and summed in bfloat16 or wider, within the bound.
A program may use at most 64 MiB of HBM per device.

```python
import math
import jax
import jax.numpy as jnp
from jax import lax

D = 1024
HID = 1024
THID = 2048
TILE = 128
TILE_ROW = 4
EPT = 128
RELS = 16
SOURCES = 8192
TARGETS = 4096
TILES = 128


def draw_tile_count(key, part):
    order_key = jax.random.fold_in(key, 101)
    live_key = jax.random.fold_in(key, 202)
    amount_key = jax.random.fold_in(key, 303)
    full_key = jax.random.fold_in(key, 404)
    order = jax.random.permutation(order_key, RELS).astype(jnp.int32)
    shift_amount = order * 3 // max(RELS - 1, 1)
    keep_level = jnp.left_shift(jnp.ones((RELS,), jnp.int32), 3 - shift_amount)
    rolled = jax.random.randint(live_key, (RELS, TILES), 0, 8)
    live_mask = rolled < keep_level[:, None]
    amount = jax.random.randint(amount_key, (RELS, TILES), EPT // 2, EPT + 1)
    counts = jnp.where(live_mask, amount, 0)
    full_at = jax.random.randint(full_key, (RELS,), 0, TILES)
    position = lax.broadcasted_iota(jnp.int32, (RELS, TILES), 1)
    return jnp.where(position == full_at[:, None], EPT, counts).astype(jnp.int32)


def touch_ends(result, key, low, top_value):
    longest = result.shape.index(max(result.shape))
    spots = []
    for shift in (0, 1):
        where = [jax.random.randint(jax.random.fold_in(key, axis), (), 0, length) for axis, length in enumerate(result.shape)]
        where[longest] = (where[longest] + shift) % result.shape[longest]
        spots.append(tuple(where))
    return result.at[spots[0]].set(low).at[spots[1]].set(top_value)


def block_levels(key, shape, shards, least, high):
    gain, own = 1.0, jax.random.fold_in(key, 6)
    for axis_at, blocks in shards:
        steps = jnp.exp(jax.random.uniform(jax.random.fold_in(own, axis_at), (blocks,), jnp.float32, least / len(shards), high / len(shards)))
        gain = gain * jnp.repeat(steps, shape[axis_at] // blocks).reshape([-1 if axis == axis_at else 1 for axis in range(len(shape))])
    return gain


def noise(key, dims, deviation, limit, split=(), kind=jnp.bfloat16):
    gain = block_levels(key, dims, split, -0.22, 0.18) if split else 1.0
    entries = jax.random.normal(key, dims, jnp.float32) * deviation * gain
    return jnp.minimum(jnp.maximum(entries, -limit), limit).astype(kind)


def setup_inputs(seed: int = 0) -> dict:
    seeds = jax.random.split(jax.random.key(seed), 12)
    return {
        "src_feat": noise(seeds[0], (RELS, SOURCES, D), 1.0, 6.0, ((0, 16), (1, 32))),
        "rel_w_in": noise(seeds[1], (RELS, D, HID), D ** -0.5, 0.1875, ((0, 16), (1, 32))),
        "rel_w_out": noise(seeds[2], (RELS, HID, D), HID ** -0.5, 0.1875, ((0, 16), (1, 32))),
        "tile_source": touch_ends(jax.random.randint(seeds[3], (RELS, TILES), 0, SOURCES // TILE), jax.random.fold_in(seeds[3], 1), 0, (SOURCES // TILE) - 1).astype(jnp.int32),
        "tile_edges": touch_ends(jax.random.randint(seeds[4], (RELS, TILES, EPT), 0, TILE * TILE), jax.random.fold_in(seeds[4], 1), 0, (TILE * TILE) - 1).astype(jnp.int32),
        "tile_count": draw_tile_count(jax.random.fold_in(seeds[11], 71), 0),
        "target_feat": noise(seeds[6], (TARGETS, D), 1.0, 6.0, ((0, 512),)),
        "norm_gain": jnp.clip(jnp.exp(jax.random.uniform(seeds[7], (D,), jnp.float32, math.log(0.5), math.log(2.0))), 0.5, 2.0),
        "tgt_w_in": noise(seeds[8], (D, THID), D ** -0.5, 0.1875, ((1, 16),)),
        "tgt_w_out": noise(seeds[9], (THID, D), THID ** -0.5, 0.125, ((0, 16),)),
        "out_grad": noise(seeds[10], (TARGETS, D), 1.0, 6.0, ((0, 512),)),
    }


eps_norm = 1e-06

def silu_slope(values):
    sigma = jax.nn.sigmoid(values)
    return sigma * (1.0 + values * (1.0 - sigma))

def tile_counts(edge_codes, live_counts):
    slots = jnp.arange(edge_codes.shape[1], dtype=jnp.int32)
    live_mask = slots[None, :] < live_counts[:, None]
    lattice = jnp.arange(TILE, dtype=jnp.int32)
    target_hot = ((edge_codes // TILE)[:, :, None] == lattice[None, None, :]) & live_mask[:, :, None]
    source_hot = (edge_codes % TILE)[:, :, None] == lattice[None, None, :]
    return jnp.einsum('kes,ket->kst', source_hot.astype(jnp.float32), target_hot.astype(jnp.float32))

def reference(src_feat, rel_w_in, rel_w_out, tile_source, tile_edges, tile_count, target_feat, norm_gain, tgt_w_in, tgt_w_out, out_grad):

    def forward_one(carry_sum, inputs):
        source_rows, weight_in, weight_out, chosen, edge_codes, live_counts = inputs
        hidden_pre = jnp.dot(source_rows, weight_in, preferred_element_type=jnp.float32)
        hidden = jax.nn.silu(hidden_pre).astype(jnp.bfloat16)
        mixed = jnp.dot(hidden, weight_out, preferred_element_type=jnp.float32).astype(jnp.bfloat16)
        counts = tile_counts(edge_codes, live_counts)
        blocks = jnp.take(mixed.astype(jnp.float32).reshape(SOURCES // TILE, TILE, D), chosen, axis=0)
        contrib = jnp.einsum('kst,ksd->ktd', counts, blocks)
        contrib = contrib.reshape(TARGETS // TILE, TILE_ROW, TILE, D).sum(axis=1).reshape(TARGETS, D)
        return (carry_sum + contrib, jnp.zeros((), jnp.float32))
    inputs = (src_feat, rel_w_in, rel_w_out, tile_source, tile_edges, tile_count)
    aggregated = lax.scan(forward_one, jnp.zeros((TARGETS, D), jnp.float32), inputs)[0]
    inverse_norm = lax.rsqrt(lax.optimization_barrier(jnp.mean(aggregated * aggregated, axis=1, keepdims=True)) + eps_norm)
    gain_row = norm_gain.astype(jnp.float32)[None, :]
    normed = (aggregated * inverse_norm * gain_row).astype(jnp.bfloat16)
    target_pre = jnp.dot(normed, tgt_w_in, preferred_element_type=jnp.float32)
    target_hidden = jax.nn.silu(target_pre).astype(jnp.bfloat16)
    update = jnp.dot(target_hidden, tgt_w_out, preferred_element_type=jnp.float32)
    updated = (target_feat.astype(jnp.float32) + update).astype(jnp.bfloat16)
    grad_hidden_t = jnp.dot(out_grad, tgt_w_out.T, preferred_element_type=jnp.float32)
    grad_pre_t = (grad_hidden_t * silu_slope(target_pre)).astype(jnp.bfloat16)
    grad_normed = jnp.dot(grad_pre_t, tgt_w_in.T, preferred_element_type=jnp.float32)
    scaled = grad_normed * gain_row
    mean_term = lax.optimization_barrier(jnp.mean(aggregated * scaled, axis=1, keepdims=True))
    grad_agg = (inverse_norm * (scaled - aggregated * inverse_norm * inverse_norm * mean_term)).astype(jnp.bfloat16)

    def backward_one(inputs):
        source_rows, weight_in, weight_out, chosen, edge_codes, live_counts = inputs
        hidden_pre = jnp.dot(source_rows, weight_in, preferred_element_type=jnp.float32)
        counts = tile_counts(edge_codes, live_counts)
        per_tile = jnp.repeat(grad_agg.astype(jnp.float32).reshape(TARGETS // TILE, TILE, D), TILE_ROW, axis=0)
        contrib = jnp.einsum('kst,ktd->ksd', counts, per_tile)
        summed = jax.ops.segment_sum(contrib, chosen, num_segments=SOURCES // TILE)
        grad_mixed = summed.reshape(SOURCES, D).astype(jnp.bfloat16)
        grad_hidden = jnp.dot(grad_mixed, weight_out.T, preferred_element_type=jnp.float32)
        grad_pre = (grad_hidden * silu_slope(hidden_pre)).astype(jnp.bfloat16)
        return jnp.dot(grad_pre, weight_in.T, preferred_element_type=jnp.float32).astype(jnp.bfloat16)
    src_grad = lax.map(backward_one, inputs)
    return (updated, src_grad)
```

```python
import functools

import jax
import jax.numpy as jnp
from jax import lax
from jax.experimental import pallas as pl
from jax.experimental.pallas import tpu as pltpu
from jax.sharding import PartitionSpec as P

TILE = 128
TILE_ROW = 4
RING_X = 4

eps_norm = 1e-06

BF = jnp.bfloat16
F32 = jnp.float32
MESH = pl.DeviceIdType.MESH


def silu_slope(values):
    sigma = jax.nn.sigmoid(values)
    return sigma * (1.0 + values * (1.0 - sigma))


def dot_nn(a, b):
    return lax.dot_general(a, b, (((1,), (0,)), ((), ())), preferred_element_type=F32)


def dot_nt(a, b):
    return lax.dot_general(a, b, (((1,), (1,)), ((), ())), preferred_element_type=F32)


def tile_tables(source_ids, source_blocks):
    total = source_ids.shape[0]
    spot = jnp.arange(total, dtype=jnp.int32)
    earlier = (source_ids[None, :] < source_ids[:, None]) | (
        (source_ids[None, :] == source_ids[:, None]) & (spot[None, :] < spot[:, None])
    )
    rank = jnp.sum(earlier.astype(jnp.int32), axis=1)
    placed = rank[:, None] == spot[None, :]
    order = jnp.sum(jnp.where(placed, spot[:, None], 0), axis=0)
    here = jnp.sum(jnp.where(placed, source_ids[:, None], 0), axis=0)
    before = jnp.sum(jnp.where(rank[:, None] + 1 == spot[None, :], source_ids[:, None] + 1, 0), axis=0) - 1
    keep = (here == before).astype(jnp.int32)
    named = source_ids[:, None] == spot[None, :]
    upto = jnp.sum((source_ids[:, None] <= spot[None, :]).astype(jnp.int32), axis=0)
    last = jnp.where(jnp.any(named, axis=0), upto - 1, total)
    return jnp.stack([order, order // TILE_ROW, keep, last])


def whole_kernel(
    DV,
    R,
    ids,
    live,
    tab,
    src,
    win,
    wout,
    edges,
    tfeat,
    gain,
    twi,
    two,
    og,
    upd_out,
    grad_out,
    w_in,
    w_out,
    pre,
    hid_t,
    hid_by_feature,
    counts,
    agg_send,
    agg_recv,
    part_send,
    part_recv,
    norm_send,
    norm_recv,
    og_send,
    og_recv,
    gn_send,
    gn_recv,
    up_send,
    up_recv,
    ga_send,
    ga_recv,
    gt_send,
    gt_recv,
    runs,
    gh_send,
    gh_recv,
    grad_pre,
    ring_sem,
    ring_send_sem,
    send_sem,
    recv_sem,
):
    D = src.shape[1]
    half_d = D // 2
    F = D // DV
    H = F // 2
    T = ids.shape[1]
    TR = tfeat.shape[0]
    X = RING_X
    Y = DV // X
    HY = Y // 2
    W = min(256, half_d)
    rd = lax.axis_index("rel")
    me = lax.axis_index("dev")
    my_y = me // X
    my_x = lax.rem(me, X)

    def at(dy, dx):
        return lax.rem(my_y + dy + Y, Y) * X + lax.rem(my_x + dx + X, X)

    barrier = pltpu.get_barrier_semaphore()

    def greet_dev(i, c):
        pl.semaphore_signal(
            barrier, inc=1, device_id={"dev": lax.rem(me + i, DV)}, device_id_type=MESH
        )
        return c

    def greet_rel(i, c):
        pl.semaphore_signal(
            barrier, inc=1, device_id={"rel": lax.rem(rd + i, R)}, device_id_type=MESH
        )
        return c

    lax.fori_loop(1, DV, greet_dev, 0)
    lax.fori_loop(1, R, greet_rel, 0)
    pl.semaphore_wait(barrier, DV + R - 2)

    full = (w_in, w_out)
    own = (win, wout)

    def rows_of(block, half):
        return pl.ds(pl.multiple_of(block * F + half * H, H), H)

    def push(w, half, block, to, own_block=False):
        rows = rows_of(block, half)
        piece = own[w].at[pl.ds(half * H, H)] if own_block else full[w].at[rows]
        pltpu.make_async_remote_copy(
            src_ref=piece,
            dst_ref=full[w].at[rows],
            send_sem=ring_send_sem.at[w],
            recv_sem=ring_sem.at[w, half, block],
            device_id={"dev": to},
            device_id_type=MESH,
        ).start()

    def arrive(w, half, block):
        piece = full[w].at[rows_of(block, half)]
        pltpu.make_async_copy(piece, piece, ring_sem.at[w, half, block]).wait()

    def begin(w):
        push(w, 0, me, at(1, 0), True)
        push(w, 0, me, at(-1, 0), True)
        push(w, 1, me, at(0, 1), True)
        push(w, 1, me, at(0, -1), True)
        push(w, 0, me, at(0, 1), True)
        push(w, 0, me, at(0, -1), True)
        push(w, 1, me, at(1, 0), True)
        push(w, 1, me, at(-1, 0), True)
        push(w, 0, me, at(0, 2), True)
        full[w][pl.ds(pl.multiple_of(me * F, F), F), :] = own[w][...]

    def relay_x(w, dy):
        y = lax.rem(my_y + dy + Y, Y)
        even = lax.rem(y, 2) == 0
        arrive(w, 1, at(dy, -1))
        arrive(w, 1, at(dy, 1))
        block = jnp.where(even, at(dy, -1), at(dy, 1))
        push(w, 1, block, jnp.where(even, at(0, 1), at(0, -1)))

    def round_of(w, s):
        if s <= HY:

            def column(i, c):
                dx = lax.rem(i * 3, X)
                if s == 0:
                    arrive(w, 0, at(0, dx))
                    push(w, 0, at(0, dx), at(1, 0))
                    push(w, 0, at(0, dx), at(-1, 0))
                elif s < HY:
                    arrive(w, 0, at(-s, dx))
                    if s < HY - 1:
                        push(w, 0, at(-s, dx), at(1, 0))
                    arrive(w, 0, at(s, dx))
                    if s < HY - 1:
                        push(w, 0, at(s, dx), at(-1, 0))
                    else:
                        even = lax.rem(my_x + dx, 2) == 0
                        push(
                            w,
                            0,
                            jnp.where(even, at(-s, dx), at(s, dx)),
                            jnp.where(even, at(1, 0), at(-1, 0)),
                        )
                else:
                    arrive(w, 0, at(HY, dx))
                return c

            lax.fori_loop(1 if s == 0 else 0, X, column, 0)
        if 1 <= s < HY:
            for d in (-s, s):
                arrive(w, 1, at(d, 0))
                if s < HY - 1:
                    push(w, 1, at(d, 0), at(1 if d < 0 else -1, 0))
                push(w, 1, at(d, 0), at(0, 1))
                push(w, 1, at(d, 0), at(0, -1))
            if s == HY - 1:
                even = lax.rem(my_x, 2) == 0
                push(
                    w,
                    1,
                    jnp.where(even, at(-s, 0), at(s, 0)),
                    jnp.where(even, at(1, 0), at(-1, 0)),
                )
        elif s == HY:
            arrive(w, 1, at(HY, 0))
            push(w, 1, at(HY, 0), at(0, 1))
            push(w, 1, at(HY, 0), at(0, -1))
        if s == 1:
            relay_x(w, 0)
        elif 2 <= s <= HY:
            relay_x(w, -(s - 1))
            relay_x(w, s - 1)
        elif s == HY + 1:
            relay_x(w, HY)
        if s == HY + 1:

            def rest(i, c):
                arrive(w, 1, i * X + lax.rem(my_x + 2, X))
                return c

            lax.fori_loop(0, Y, rest, 0)

    ROUNDS = HY + 2

    def over_dev(n, piece, place):
        def send(i, c):
            to = lax.rem(me + i, DV)
            pltpu.make_async_remote_copy(
                src_ref=piece(to),
                dst_ref=place,
                send_sem=send_sem.at[n],
                recv_sem=recv_sem.at[n],
                device_id={"dev": to},
                device_id_type=MESH,
            ).start()
            return c

        lax.fori_loop(1, DV, send, 0)

    def over_rel(n, piece, place):
        def send(i, c):
            to = lax.rem(rd + i, R)
            pltpu.make_async_remote_copy(
                src_ref=piece(to),
                dst_ref=place,
                send_sem=send_sem.at[n],
                recv_sem=recv_sem.at[n],
                device_id={"rel": to},
                device_id_type=MESH,
            ).start()
            return c

        lax.fori_loop(1, R, send, 0)

    def all_of(sem, view):
        pltpu.make_async_copy(view, view, sem).wait()

    def folded(rows):
        return jnp.concatenate([rows[..., :half_d], rows[..., half_d:]], axis=-2).astype(BF)

    def block_rows(buffer):
        held = buffer[...].astype(F32)
        rows = jnp.concatenate([held[:, :TR, :], held[:, TR:, :]], axis=2)
        return rows.reshape(R * TR, D).astype(BF)

    def own_sum(buffer):
        total = buffer[0].astype(F32)
        for r in range(1, R):
            total = total + buffer[r].astype(F32)
        return jnp.concatenate([total[:TR], total[TR:]], axis=1)

    def count_tiles(first, number):
        lattice = lax.broadcasted_iota(jnp.int32, (TILE, TILE), 0)
        slots = lax.broadcasted_iota(jnp.int32, (1, TILE), 1)

        def some(i, c):
            for u in range(4):
                k = first + i * 4 + u
                codes = edges[pl.ds(k, 1), :]
                s_at = jnp.bitwise_and(codes, TILE - 1)
                t_at = jnp.where(slots < live[0, k], jnp.right_shift(codes, 7), -1)
                s_hot = (lattice == s_at).astype(F32).astype(BF)
                t_hot = (lattice == t_at).astype(F32).astype(BF)
                counts[k] = dot_nt(s_hot, t_hot).astype(BF)
            return c

        lax.fori_loop(0, number // 4, some, 0)

    begin(0)
    og_send[...] = folded(og[...].astype(F32))
    og_recv[rd] = og_send[...]
    over_rel(0, lambda to: og_send, og_recv.at[rd])
    share = T // 8
    for s in range(ROUNDS):
        count_tiles(s * share, share)
        round_of(0, s)
    begin(1)

    def first_projection(j, c):
        cols = pl.ds(pl.multiple_of(j * W, W), W)
        value = dot_nn(src[...], w_in[:, cols])
        pre[:, cols] = value
        turned = (value * jax.nn.sigmoid(value)).T.astype(BF)
        hid_t[0, cols, :] = turned[:, :TILE]
        hid_t[1, cols, :] = turned[:, TILE:]
        return c

    lax.fori_loop(0, D // W, first_projection, 0)
    over_dev(
        1,
        lambda to: hid_t.at[:, pl.ds(pl.multiple_of(to * F, F), F), :],
        hid_by_feature.at[pl.ds(2 * me, 2)],
    )
    hid_by_feature[pl.ds(2 * me, 2)] = hid_t[:, pl.ds(pl.multiple_of(me * F, F), F), :]
    early = HY
    for s in range(early):
        if s == 0:
            count_tiles(ROUNDS * share, T - ROUNDS * share)
        round_of(1, s)
    all_of(recv_sem.at[0], og_recv.at[pl.ds(0, R - 1)])
    grad_hidden_t = dot_nt(block_rows(og_recv), two[...])

    all_of(recv_sem.at[1], hid_by_feature.at[pl.ds(0, 2 * (DV - 1))])

    def aggregate(i, c):
        for u in range(4):
            b = i * 4 + u
            total = jnp.zeros((F, TILE), F32)
            for q in range(TILE_ROW):
                k = b * TILE_ROW + q
                total = total + dot_nn(hid_by_feature[ids[0, k]], counts[k])
            agg_send[b] = total.astype(BF)
        return c

    lax.fori_loop(0, T // TILE_ROW // 4, aggregate, 0)
    my_rows = pl.ds(pl.multiple_of(me * F, F), F)
    over_dev(2, lambda to: agg_send.at[to], agg_recv.at[my_rows])
    agg_recv[my_rows, :] = agg_send[me]
    for s in range(early, ROUNDS):
        round_of(1, s)
    all_of(recv_sem.at[2], agg_recv.at[pl.ds(0, D - F)])

    agg_hidden = agg_recv[...].astype(F32).T.astype(BF)
    for j in range(half_d // W):
        low = dot_nn(agg_hidden, w_out[:, j * W : (j + 1) * W])
        high = dot_nn(agg_hidden, w_out[:, half_d + j * W : half_d + (j + 1) * W])
        both = jnp.concatenate([low.reshape(R, TR, W), high.reshape(R, TR, W)], axis=1)
        part_send[:, :, j * W : (j + 1) * W] = both.astype(BF)
    over_rel(3, lambda to: part_send.at[to], part_recv.at[rd])
    part_recv[rd] = part_send[rd]
    all_of(recv_sem.at[3], part_recv.at[pl.ds(0, R - 1)])
    agg = own_sum(part_recv)
    gain_row = gain[...]
    inverse_norm = lax.rsqrt(jnp.mean(agg * agg, axis=1, keepdims=True) + eps_norm)
    norm_send[...] = folded(agg * inverse_norm * gain_row)
    over_rel(4, lambda to: norm_send, norm_recv.at[rd])
    norm_recv[rd] = norm_send[...]
    all_of(recv_sem.at[4], norm_recv.at[pl.ds(0, R - 1)])
    target_pre = dot_nn(block_rows(norm_recv), twi[...])
    grad_pre_t = (grad_hidden_t * silu_slope(target_pre)).astype(BF)
    gn_send[...] = folded(dot_nt(grad_pre_t, twi[...]).reshape(R, TR, D))
    over_rel(5, lambda to: gn_send.at[to], gn_recv.at[rd])
    gn_recv[rd] = gn_send[rd]
    target_hidden = (target_pre * jax.nn.sigmoid(target_pre)).astype(BF)
    up_send[...] = folded(dot_nn(target_hidden, two[...]).reshape(R, TR, D))
    all_of(recv_sem.at[5], gn_recv.at[pl.ds(0, R - 1)])
    scaled = own_sum(gn_recv) * gain_row
    mean_term = jnp.mean(agg * scaled, axis=1, keepdims=True)
    ga_send[...] = folded(
        inverse_norm * (scaled - agg * inverse_norm * inverse_norm * mean_term)
    )
    over_rel(7, lambda to: ga_send, ga_recv.at[rd])
    over_rel(6, lambda to: up_send.at[to], up_recv.at[rd])
    ga_recv[rd] = ga_send[...]
    up_recv[rd] = up_send[rd]
    all_of(recv_sem.at[7], ga_recv.at[pl.ds(0, R - 1)])

    grad_agg = block_rows(ga_recv)
    for j in range(D // W):
        value = dot_nt(grad_agg, w_out[j * W : (j + 1) * W, :])
        gt_send[j * W : (j + 1) * W, :] = value.T.astype(BF)
    over_dev(
        8, lambda to: gt_send.at[pl.ds(pl.multiple_of(to * F, F), F)], gt_recv.at[me]
    )
    gt_recv[me] = gt_send[my_rows, :]
    runs[T] = jnp.zeros((F, TILE), F32)
    all_of(recv_sem.at[8], gt_recv.at[pl.ds(0, DV - 1)])

    def spread(i, running):
        for u in range(8):
            j = i * 8 + u
            term = dot_nt(gt_recv[tab[1, j]], counts[tab[0, j]])
            running = running * tab[2, j].astype(F32) + term
            runs[j] = running
        return running

    lax.fori_loop(0, T // 8, spread, jnp.zeros((F, TILE), F32))

    def settle(i, c):
        for u in range(8):
            b = i * 8 + u
            gh_send[b] = runs[tab[3, b]].astype(BF)
        return c

    lax.fori_loop(0, 2 * DV // 8, settle, 0)
    over_dev(9, lambda to: gh_send.at[pl.ds(2 * to, 2)], gh_recv.at[:, my_rows, :])
    gh_recv[:, my_rows, :] = gh_send[pl.ds(2 * me, 2)]

    all_of(recv_sem.at[6], up_recv.at[pl.ds(0, R - 1)])
    upd_out[...] = (tfeat[...].astype(F32) + own_sum(up_recv)).astype(BF)
    for w in range(2):
        all_of(ring_send_sem.at[w], full[w].at[pl.ds(0, D - F)])
    all_of(send_sem.at[1], hid_by_feature.at[pl.ds(0, 2 * (DV - 1))])
    all_of(send_sem.at[2], agg_recv.at[pl.ds(0, D - F)])
    for n, held in (
        (0, og_recv),
        (3, part_recv),
        (4, norm_recv),
        (5, gn_recv),
        (6, up_recv),
        (7, ga_recv),
    ):
        all_of(send_sem.at[n], held.at[pl.ds(0, R - 1)])
    all_of(send_sem.at[8], gt_recv.at[pl.ds(0, DV - 1)])

    all_of(recv_sem.at[9], gh_recv.at[:, pl.ds(0, D - F), :])

    def last_slope(j, c):
        cols = pl.ds(pl.multiple_of(j * W, W), W)
        turned = jnp.concatenate([gh_recv[0, cols, :], gh_recv[1, cols, :]], axis=1)
        value = turned.astype(F32).T * silu_slope(pre[:, cols])
        grad_pre[:, cols] = value.astype(BF)
        return c

    lax.fori_loop(0, D // W, last_slope, 0)

    def last_projection(j, c):
        cols = pl.ds(pl.multiple_of(j * W, W), W)
        grad_out[:, cols] = dot_nt(grad_pre[...], w_in[cols, :]).astype(BF)
        return c

    lax.fori_loop(0, D // W, last_projection, 0)
    all_of(send_sem.at[9], gh_recv.at[:, pl.ds(0, D - F), :])


def shards(
    src_feat,
    rel_w_in,
    rel_w_out,
    tile_source,
    tile_edges,
    tile_count,
    target_feat,
    norm_gain,
    tgt_w_in,
    tgt_w_out,
    out_grad,
):
    DV = lax.axis_size("dev")
    R = lax.axis_size("rel")
    own_rows = src_feat[0]
    rows, D = own_rows.shape
    F = D // DV
    T = tile_source.shape[1]
    TR = target_feat.shape[0]
    tables = tile_tables(tile_source[0], rows * DV // TILE)

    vmem = pl.BlockSpec(memory_space=pltpu.VMEM)
    smem = pl.BlockSpec(memory_space=pltpu.SMEM)
    piece = pltpu.VMEM((2 * TR, D // 2), BF)
    pieces = pltpu.VMEM((R, 2 * TR, D // 2), BF)
    updated, grad_source = pl.pallas_call(
        functools.partial(whole_kernel, DV, R),
        out_shape=(
            jax.ShapeDtypeStruct((TR, D), BF),
            jax.ShapeDtypeStruct((rows, D), BF),
        ),
        in_specs=[smem] * 3 + [vmem] * 9,
        out_specs=(vmem, vmem),
        scratch_shapes=[
            pltpu.VMEM((D, D), BF),
            pltpu.VMEM((D, D), BF),
            pltpu.VMEM((rows, D), F32),
            pltpu.VMEM((2, D, TILE), BF),
            pltpu.VMEM((2 * DV, F, TILE), BF),
            pltpu.VMEM((T, TILE, TILE), BF),
            pltpu.VMEM((DV, F, TILE), BF),
            pltpu.VMEM((D, TILE), BF),
            pieces,
            pieces,
            piece,
            pieces,
            piece,
            pieces,
            pieces,
            pieces,
            pieces,
            pieces,
            piece,
            pieces,
            pltpu.VMEM((D, TILE), BF),
            pltpu.VMEM((DV, F, TILE), BF),
            pltpu.VMEM((T + 1, F, TILE), F32),
            pltpu.VMEM((2 * DV, F, TILE), BF),
            pltpu.VMEM((2, D, TILE), BF),
            pltpu.VMEM((rows, D), BF),
            pltpu.SemaphoreType.DMA((2, 2, DV)),
            pltpu.SemaphoreType.DMA((2,)),
            pltpu.SemaphoreType.DMA((10,)),
            pltpu.SemaphoreType.DMA((10,)),
        ],
        compiler_params=pltpu.CompilerParams(
            collective_id=0, has_side_effects=True, vmem_limit_bytes=60 * 1024 * 1024
        ),
        name="whole_layer",
    )(
        tile_source,
        tile_count,
        tables,
        own_rows,
        rel_w_in[0],
        rel_w_out[0],
        tile_edges[0],
        target_feat,
        norm_gain[None, :],
        tgt_w_in,
        tgt_w_out,
        out_grad,
    )
    return (updated, grad_source[None])


def solution(mesh):
    placed = (
        P("rel", "dev", None),
        P("rel", "dev", None),
        P("rel", "dev", None),
        P("rel", None),
        P("rel", None, None),
        P("rel", None),
        P(("dev", "rel"), None),
        P(),
        P(None, "rel"),
        P("rel", None),
        P(("dev", "rel"), None),
    )
    return jax.shard_map(
        shards,
        mesh=mesh,
        in_specs=placed,
        out_specs=(P(("dev", "rel"), None), P("rel", "dev", None)),
        check_vma=False,
    )
```

```python
import functools

import jax
import jax.numpy as jnp
from jax import lax
from jax.experimental import pallas as pl
from jax.experimental.pallas import tpu as pltpu
from jax.sharding import PartitionSpec as P

TILE = 128
TILE_ROW = 4
RING_X = 4

eps_norm = 1e-06

BF = jnp.bfloat16
F32 = jnp.float32
MESH = pl.DeviceIdType.MESH


def silu_slope(values):
    sigma = jax.nn.sigmoid(values)
    return sigma * (1.0 + values * (1.0 - sigma))


def dot_nn(a, b):
    return lax.dot_general(a, b, (((1,), (0,)), ((), ())), preferred_element_type=F32)


def dot_nt(a, b):
    return lax.dot_general(a, b, (((1,), (1,)), ((), ())), preferred_element_type=F32)


def tile_tables(source_ids, source_blocks):
    total = source_ids.shape[0]
    spot = jnp.arange(total, dtype=jnp.int32)
    earlier = (source_ids[None, :] < source_ids[:, None]) | (
        (source_ids[None, :] == source_ids[:, None]) & (spot[None, :] < spot[:, None])
    )
    rank = jnp.sum(earlier.astype(jnp.int32), axis=1)
    placed = rank[:, None] == spot[None, :]
    order = jnp.sum(jnp.where(placed, spot[:, None], 0), axis=0)
    here = jnp.sum(jnp.where(placed, source_ids[:, None], 0), axis=0)
    before = jnp.sum(jnp.where(rank[:, None] + 1 == spot[None, :], source_ids[:, None] + 1, 0), axis=0) - 1
    keep = (here == before).astype(jnp.int32)
    named = source_ids[:, None] == spot[None, :]
    upto = jnp.sum((source_ids[:, None] <= spot[None, :]).astype(jnp.int32), axis=0)
    last = jnp.where(jnp.any(named, axis=0), upto - 1, total)
    return jnp.stack([order, order // TILE_ROW, keep, last])


def whole_kernel(
    DV,
    R,
    ids,
    live,
    tab,
    src_in,
    win_in,
    wout_in,
    edges_in,
    tfeat,
    gain,
    twi_in,
    two_in,
    og,
    upd_out,
    grad_out,
    src,
    edges,
    w_a,
    w_b,
    w_out,
    twi,
    two,
    pre,
    hid_t,
    hid_by_feature,
    counts,
    agg_send,
    agg_recv,
    part_send,
    part_pair,
    part_sum,
    part_recv,
    ga_send,
    ga_recv,
    gt_send,
    gt_recv,
    runs,
    gh_send,
    gh_recv,
    grad_pre,
    copy_sem,
    ring_sem,
    ring_send_sem,
    y_sem,
    x_sem,
    far_sem,
    wout_send_sem,
    z_sem,
    z_send_sem,
    ga_sem,
    send_sem,
    recv_sem,
):
    D = src.shape[1]
    HD = D // 2
    F = D // DV
    T = ids.shape[1]
    TR = tfeat.shape[0]
    X = RING_X
    Y = DV // X
    HY = Y // 2
    Z = R // 2
    HZ = Z // 2
    W = min(256, HD)
    rd = lax.axis_index("rel")
    me = lax.axis_index("dev")
    my_y = me // X
    my_x = lax.rem(me, X)
    my_z = rd // 2
    my_c = lax.rem(rd, 2)

    def take(n, source, place):
        copy = pltpu.make_async_copy(source, place, copy_sem.at[n])
        copy.start()
        return copy

    own_a = take(0, win_in.at[:, pl.ds(0, HD)], w_a.at[me])
    own_b = take(1, win_in.at[:, pl.ds(HD, HD)], w_b.at[me])
    own_twi = take(2, twi_in, twi.at[rd])
    own_two = take(3, two_in, two.at[rd])
    own_out = take(4, wout_in, w_out.at[my_y, my_x])
    own_src = take(5, src_in, src)
    own_edges = take(6, edges_in, edges)

    def col(dx):
        return lax.rem(my_x + dx + X, X)

    def row(dy):
        return lax.rem(my_y + dy + Y, Y)

    def at(dy, dx):
        return row(dy) * X + col(dx)

    def zc(dz, dc=0):
        return lax.rem(my_z + dz + Z, Z) * 2 + lax.rem(my_c + dc, 2)

    barrier = pltpu.get_barrier_semaphore()

    def greet_dev(i, c):
        pl.semaphore_signal(
            barrier, inc=1, device_id={"dev": lax.rem(me + i, DV)}, device_id_type=MESH
        )
        return c

    def greet_rel(i, c):
        pl.semaphore_signal(
            barrier, inc=1, device_id={"rel": lax.rem(rd + i, R)}, device_id_type=MESH
        )
        return c

    lax.fori_loop(1, DV, greet_dev, 0)
    lax.fori_loop(1, R, greet_rel, 0)
    for copy in (own_a, own_b, own_twi, own_two, own_out, own_src, own_edges):
        copy.wait()
    pl.semaphore_wait(barrier, DV + R - 2)

    def remote(piece, place, sent, got, axis, to):
        pltpu.make_async_remote_copy(
            src_ref=piece,
            dst_ref=place,
            send_sem=sent,
            recv_sem=got,
            device_id={axis: to},
            device_id_type=MESH,
        ).start()

    def all_of(sem, view):
        pltpu.make_async_copy(view, view, sem).wait()

    half = (w_a, w_b)

    def push(h, block, to):
        piece = half[h].at[block]
        remote(piece, piece, ring_send_sem.at[h], ring_sem.at[h, block], "dev", to)

    def arrive(h, block):
        all_of(ring_sem.at[h, block], half[h].at[block])

    def begin_in():
        push(0, me, at(1, 0))
        push(0, me, at(-1, 0))
        push(0, me, at(0, 1))
        push(0, me, at(0, -1))
        push(1, me, at(1, 0))
        push(1, me, at(-1, 0))
        push(0, me, at(0, 2))
        push(1, me, at(0, 1))
        push(1, me, at(0, -1))

    def relay_x(dy):
        even = lax.rem(row(dy), 2) == 0
        arrive(1, at(dy, -1))
        arrive(1, at(dy, 1))
        push(
            1,
            jnp.where(even, at(dy, -1), at(dy, 1)),
            jnp.where(even, at(0, 1), at(0, -1)),
        )

    def first_half(s):
        def column(i, c):
            dx = jnp.where(i == 3, 2, jnp.where(i == 2, 3, i))
            if s == 0:
                arrive(0, at(0, dx))
                push(0, at(0, dx), at(1, 0))
                push(0, at(0, dx), at(-1, 0))
            elif s < HY:
                arrive(0, at(-s, dx))
                if s < HY - 1:
                    push(0, at(-s, dx), at(1, 0))
                arrive(0, at(s, dx))
                if s < HY - 1:
                    push(0, at(s, dx), at(-1, 0))
                else:
                    even = lax.rem(my_x + dx, 2) == 0
                    push(
                        0,
                        jnp.where(even, at(-s, dx), at(s, dx)),
                        jnp.where(even, at(1, 0), at(-1, 0)),
                    )
            else:
                arrive(0, at(HY, dx))
            return c

        lax.fori_loop(1 if s == 0 else 0, X, column, 0)

    def to_row(dy, far):
        push(1, at(dy, 0), at(0, 1))
        push(1, at(dy, 0), at(0, -1))
        if far:
            push(1, at(dy, 0), at(0, 2))

    def second_half(s):
        far = s >= HY - 1
        if 1 <= s < HY:
            for d in (-s, s):
                arrive(1, at(d, 0))
                if s < HY - 1:
                    push(1, at(d, 0), at(1 if d < 0 else -1, 0))
            if s == HY - 1:
                even = lax.rem(my_x, 2) == 0
                push(
                    1,
                    jnp.where(even, at(-s, 0), at(s, 0)),
                    jnp.where(even, at(1, 0), at(-1, 0)),
                )
            for d in (-s, s):
                to_row(d, far)
        elif s == HY:
            arrive(1, at(HY, 0))
            to_row(HY, far)
        if s == 1:
            relay_x(0)
        elif 2 <= s < HY:
            relay_x(-(s - 1))
            relay_x(s - 1)

    def second_rest():
        for d in (-(HY - 1), HY - 1, HY):
            arrive(1, at(d, 1))
            arrive(1, at(d, -1))
        if HY == 2:
            pass

        def rest(i, c):
            arrive(1, i * X + col(2))
            return c

        lax.fori_loop(0, Y, rest, 0)

    def out_push(y, to):
        piece = w_out.at[y, my_x]
        remote(piece, piece, wout_send_sem.at[0], y_sem.at[y], "dev", to)

    def out_arrive(y):
        all_of(y_sem.at[y], w_out.at[y, my_x])

    def out_y(s):
        if s == 0:
            out_push(my_y, at(1, 0))
            out_push(my_y, at(-1, 0))
        elif s < HY:
            out_arrive(row(-s))
            if s < HY - 1:
                out_push(row(-s), at(1, 0))
            out_arrive(row(s))
            if s < HY - 1:
                out_push(row(s), at(-1, 0))
            else:
                even = lax.rem(my_x, 2) == 0
                out_push(
                    jnp.where(even, row(-s), row(s)), jnp.where(even, at(1, 0), at(-1, 0))
                )
        else:
            out_arrive(row(HY))

    def out_part(c, x):
        return w_out.at[pl.ds(c * HY, HY), x]

    def out_x_begin():
        for side, c in ((0, 0), (1, 1), (0, 1), (1, 0)):
            piece = out_part(c, my_x)
            to = at(0, 1) if side == 0 else at(0, -1)
            remote(piece, piece, wout_send_sem.at[1], x_sem.at[side, c], "dev", to)

    def out_x_relay():
        for side in (0, 1):
            piece = out_part(side, col(-1) if side == 0 else col(1))
            all_of(x_sem.at[side, side], piece)
            to = at(0, 1) if side == 0 else at(0, -1)
            remote(piece, piece, wout_send_sem.at[1], far_sem.at[side], "dev", to)

    def out_x_rest():
        for side in (0, 1):
            all_of(x_sem.at[side, 1 - side], out_part(1 - side, col(-1) if side == 0 else col(1)))
        for side in (0, 1):
            all_of(far_sem.at[side], out_part(side, col(2)))

    tgt = (twi, two)

    def z_push(w, r, to):
        piece = tgt[w].at[r]
        remote(piece, piece, z_send_sem.at[w], z_sem.at[w, r], "rel", to)

    def z_arrive(w, r):
        all_of(z_sem.at[w, r], tgt[w].at[r])

    def z_step(s):
        for w in (0, 1):
            if s == 0:
                z_push(w, rd, zc(1))
                z_push(w, rd, zc(-1))
                z_push(w, rd, zc(0, 1))
            elif s < HZ:
                z_arrive(w, zc(-s))
                if s < HZ - 1 or w == 0:
                    z_push(w, zc(-s), zc(1))
                z_arrive(w, zc(s))
                if s < HZ - 1 or w == 1:
                    z_push(w, zc(s), zc(-1))
                z_push(w, zc(-s), zc(0, 1))
                z_push(w, zc(s), zc(0, 1))
            elif s == HZ:
                z_arrive(w, zc(HZ))
                z_push(w, zc(HZ), zc(0, 1))
            else:
                for d in range(Z):
                    z_arrive(w, zc(d, 1))

    def over_dev(n, piece, place, first=0, last=None):
        def send(i, c):
            to = lax.rem(me + i, DV)
            remote(piece(to), place, send_sem.at[n], recv_sem.at[n], "dev", to)
            return c

        lax.fori_loop(1, DV, send, 0)

    def folded(rows):
        return jnp.concatenate([rows[..., :HD], rows[..., HD:]], axis=-2).astype(BF)

    def count_tiles(first, number):
        lattice = lax.broadcasted_iota(jnp.int32, (TILE, TILE), 0).astype(F32).astype(BF)
        slots = lax.broadcasted_iota(jnp.int32, (1, TILE), 1)
        one = jnp.ones((TILE, TILE), BF)
        none = jnp.zeros((TILE, TILE), BF)

        def hot(spots):
            rows = jnp.broadcast_to(spots.astype(F32), (16, TILE)).astype(BF)
            return jnp.where(lattice == jnp.concatenate([rows] * (TILE // 16), axis=0), one, none)

        def some(i, c):
            for u in range(8):
                k = first + i * 8 + u
                codes = edges[pl.ds(k, 1), :]
                s_at = jnp.bitwise_and(codes, TILE - 1)
                t_at = jnp.where(slots < live[0, k], jnp.right_shift(codes, 7), -1)
                counts[k] = dot_nt(hot(s_at), hot(t_at)).astype(BF)
            return c

        lax.fori_loop(0, number // 8, some, 0)

    def slice_of(p):
        x = lax.rem(p, X)
        return (x // 2) * (DV // 2) + (p // X) * 2 + lax.rem(x, 2)

    mine = slice_of(me)
    my_rows = pl.ds(pl.multiple_of(mine * F, F), F)

    def rows_for(p):
        return pl.ds(pl.multiple_of(slice_of(p) * F, F), F)

    def first_projection(h):
        def some(j, c):
            cols = pl.ds(pl.multiple_of(j * W, W), W)
            value = dot_nn(src[...], half[h][:, :, cols].reshape(D, W))
            there = pl.ds(pl.multiple_of(h * HD + j * W, W), W)
            pre[:, there] = value
            turned = (value * jax.nn.sigmoid(value)).T.astype(BF)
            hid_t[0, there, :] = turned[:, :TILE]
            hid_t[1, there, :] = turned[:, TILE:]
            return c

        lax.fori_loop(0, HD // W, some, 0)

        def send(i, c):
            dy = i // 2
            to = row(dy) * X + 2 * h + lax.rem(my_x + lax.rem(i, 2), 2)

            @pl.when(to != me)
            def _():
                remote(
                    hid_t.at[:, rows_for(to), :],
                    hid_by_feature.at[pl.ds(2 * me, 2)],
                    send_sem.at[1],
                    recv_sem.at[1],
                    "dev",
                    to,
                )

            return c

        lax.fori_loop(0, DV // 2, send, 0)

    begin_in()
    z_step(0)
    for s in range(HY + 1):
        first_half(s)
        second_half(s)
        if s == HY - 1:
            z_step(1)
        if s != 1:
            out_y(max(s - 1, 0))
    first_projection(0)
    out_y(HY)
    second_rest()
    first_projection(1)
    hid_by_feature[pl.ds(2 * me, 2)] = hid_t[:, my_rows, :]
    out_x_begin()
    count_tiles(0, T)
    z_step(2)
    out_x_relay()
    all_of(recv_sem.at[1], hid_by_feature.at[pl.ds(0, 2 * (DV - 1))])

    def aggregate(i, c):
        for u in range(8):
            b = i * 8 + u
            total = jnp.zeros((F, TILE), F32)
            for q in range(TILE_ROW):
                k = b * TILE_ROW + q
                total = total + dot_nn(hid_by_feature[ids[0, k]], counts[k])
            agg_send[b] = total.astype(BF)
        return c

    lax.fori_loop(0, T // TILE_ROW // 8, aggregate, 0)
    over_dev(2, lambda to: agg_send.at[to], agg_recv.at[my_rows])
    agg_recv[my_rows, :] = agg_send[me]
    if HZ > 3:
        z_step(3)
    out_x_rest()
    all_of(recv_sem.at[2], agg_recv.at[pl.ds(0, D - F)])

    agg_hidden = agg_recv[...].astype(F32).T.astype(BF)
    for j in range(HD // W):
        low = dot_nn(agg_hidden, w_out[:, :, :, j * W : (j + 1) * W].reshape(D, W))
        high = dot_nn(agg_hidden, w_out[:, :, :, HD + j * W : HD + (j + 1) * W].reshape(D, W))
        both = jnp.concatenate([low.reshape(R, TR, W), high.reshape(R, TR, W)], axis=1)
        both = both.astype(BF).reshape(Z, 2, 2 * TR, W)
        part_send[0, :, :, j * W : (j + 1) * W] = both[:, 0]
        part_send[1, :, :, j * W : (j + 1) * W] = both[:, 1]
    remote(part_send.at[1 - my_c], part_pair, send_sem.at[0], recv_sem.at[0], "rel", zc(0, 1))
    if HZ > 2:
        z_step(HZ)

    def wide(rows):
        return (jnp.concatenate([rows, rows], axis=0) if TR < 16 else rows).astype(BF)

    all_of(recv_sem.at[0], part_pair)
    part_sum[...] = (part_send[my_c].astype(F32) + part_pair[...].astype(F32)).astype(BF)
    for d in range(1, Z):
        remote(
            part_sum.at[lax.rem(my_z + d, Z)],
            part_recv.at[my_z],
            send_sem.at[3],
            recv_sem.at[3],
            "rel",
            zc(d),
        )
    part_recv[my_z] = part_sum[my_z]
    z_step(HZ + 1)
    og_rows = wide(og[...].astype(F32))
    grad_hidden_t = [dot_nt(og_rows, two[r]) for r in range(R)]
    all_of(recv_sem.at[3], part_recv.at[pl.ds(0, Z - 1)])
    total = part_recv[0].astype(F32)
    for z in range(1, Z):
        total = total + part_recv[z].astype(F32)
    agg = jnp.concatenate([total[:TR], total[TR:]], axis=1)
    gain_row = gain[...]
    inverse_norm = lax.rsqrt(jnp.mean(agg * agg, axis=1, keepdims=True) + eps_norm)
    normed = wide(agg * inverse_norm * gain_row)
    target_pre = [dot_nn(normed, twi[r]) for r in range(R)]
    grad_normed = jnp.zeros((normed.shape[0], D), F32)
    for r in range(R):
        grad_pre_t = (grad_hidden_t[r] * silu_slope(target_pre[r])).astype(BF)
        grad_normed = grad_normed + dot_nt(grad_pre_t, twi[r])
    scaled = grad_normed[:TR] * gain_row
    mean_term = jnp.mean(agg * scaled, axis=1, keepdims=True)
    ga_send[...] = folded(
        inverse_norm * (scaled - agg * inverse_norm * inverse_norm * mean_term)
    )
    for dz in sorted(range(1, Z), key=lambda d: min(d, Z - d)):
        remote(ga_send, ga_recv.at[rd], send_sem.at[4], ga_sem.at[rd], "rel", zc(dz))
    remote(ga_send, ga_recv.at[rd], send_sem.at[4], ga_sem.at[rd], "rel", zc(0, 1))
    ga_recv[rd] = ga_send[...]
    update = jnp.zeros((normed.shape[0], D), F32)
    for r in range(R):
        target_hidden = (target_pre[r] * jax.nn.sigmoid(target_pre[r])).astype(BF)
        update = update + dot_nn(target_hidden, two[r])
    upd_out[...] = (tfeat[...].astype(F32) + update[:TR]).astype(BF)
    for dz in sorted(range(1, Z), key=lambda d: min(d, Z - d)):
        r = zc(dz)
        all_of(ga_sem.at[r], ga_recv.at[r])
        remote(ga_recv.at[r], ga_recv.at[r], send_sem.at[4], ga_sem.at[r], "rel", zc(0, 1))
    for dz in range(Z):
        r = zc(dz, 1)
        all_of(ga_sem.at[r], ga_recv.at[r])

    held = ga_recv[...].astype(F32)
    held = jnp.concatenate([held[:, :TR, :], held[:, TR:, :]], axis=2)
    grad_agg = held.reshape(R * TR, D).astype(BF)
    blocks = W // F
    for j in range(D // W):
        value = dot_nt(grad_agg, w_out[j * blocks // X : (j + 1) * blocks // X].reshape(W, D))
        gt_send[j * W : (j + 1) * W, :] = value.T.astype(BF)
    over_dev(5, lambda to: gt_send.at[rows_for(to)], gt_recv.at[me])
    gt_recv[me] = gt_send[my_rows, :]
    runs[T] = jnp.zeros((F, TILE), F32)
    all_of(recv_sem.at[5], gt_recv.at[pl.ds(0, DV - 1)])

    def spread(i, running):
        for u in range(32):
            j = i * 32 + u
            term = dot_nt(gt_recv[tab[1, j]], counts[tab[0, j]])
            running = running * tab[2, j].astype(F32) + term
            runs[j] = running
        return running

    lax.fori_loop(0, T // 32, spread, jnp.zeros((F, TILE), F32))

    def settle(i, c):
        for u in range(8):
            b = i * 8 + u
            gh_send[b] = runs[tab[3, b]].astype(BF)
        return c

    lax.fori_loop(0, 2 * DV // 8, settle, 0)
    over_dev(6, lambda to: gh_send.at[pl.ds(2 * to, 2)], gh_recv.at[:, my_rows, :])
    gh_recv[:, my_rows, :] = gh_send[pl.ds(2 * me, 2)]

    for h in range(2):
        all_of(ring_send_sem.at[h], half[h].at[pl.ds(0, DV - 1)])
        all_of(z_send_sem.at[h], tgt[h].at[pl.ds(0, R - 1)])
    all_of(wout_send_sem.at[0], w_out.at[pl.ds(0, Y - 1), 0])
    all_of(wout_send_sem.at[1], w_out.at[:, pl.ds(0, 3)])
    all_of(send_sem.at[0], part_pair)
    all_of(send_sem.at[1], hid_by_feature.at[pl.ds(0, 2 * (DV - 1))])
    all_of(send_sem.at[2], agg_recv.at[pl.ds(0, D - F)])
    all_of(send_sem.at[3], part_recv.at[pl.ds(0, Z - 1)])
    all_of(send_sem.at[4], ga_recv.at[pl.ds(0, R - 1)])
    all_of(send_sem.at[5], gt_recv.at[pl.ds(0, DV - 1)])

    all_of(recv_sem.at[6], gh_recv.at[:, pl.ds(0, D - F), :])

    def last_slope(j, c):
        cols = pl.ds(pl.multiple_of(j * W, W), W)
        turned = jnp.concatenate([gh_recv[0, cols, :], gh_recv[1, cols, :]], axis=1)
        value = turned.astype(F32).T * silu_slope(pre[:, cols])
        grad_pre[:, cols] = value.astype(BF)
        return c

    lax.fori_loop(0, D // W, last_slope, 0)

    def last_projection(j, c):
        cols = pl.ds(pl.multiple_of(j * W, W), W)
        these = pl.ds(j * blocks, blocks)
        value = dot_nt(grad_pre[:, :HD], w_a[these].reshape(W, HD))
        value = value + dot_nt(grad_pre[:, HD:], w_b[these].reshape(W, HD))
        grad_out[:, cols] = value.astype(BF)
        return c

    lax.fori_loop(0, D // W, last_projection, 0)
    all_of(send_sem.at[6], gh_recv.at[:, pl.ds(0, D - F), :])


def shards(
    src_feat,
    rel_w_in,
    rel_w_out,
    tile_source,
    tile_edges,
    tile_count,
    target_feat,
    norm_gain,
    tgt_w_in,
    tgt_w_out,
    out_grad,
):
    DV = lax.axis_size("dev")
    R = lax.axis_size("rel")
    own_rows = src_feat[0]
    rows, D = own_rows.shape
    F = D // DV
    T = tile_source.shape[1]
    TR = target_feat.shape[0]
    X, Y, Z = RING_X, DV // RING_X, R // 2
    HT = tgt_w_in.shape[1]
    tables = tile_tables(tile_source[0], rows * DV // TILE)

    vmem = pl.BlockSpec(memory_space=pltpu.VMEM)
    smem = pl.BlockSpec(memory_space=pltpu.SMEM)
    hbm = pl.BlockSpec(memory_space=pl.ANY)
    updated, grad_source = pl.pallas_call(
        functools.partial(whole_kernel, DV, R),
        out_shape=(
            jax.ShapeDtypeStruct((TR, D), BF),
            jax.ShapeDtypeStruct((rows, D), BF),
        ),
        in_specs=[smem] * 3 + [hbm] * 4 + [vmem] * 2 + [hbm] * 2 + [vmem],
        out_specs=(vmem, vmem),
        scratch_shapes=[
            pltpu.VMEM((rows, D), BF),
            pltpu.VMEM((T, TILE), jnp.int32),
            pltpu.VMEM((DV, F, D // 2), BF),
            pltpu.VMEM((DV, F, D // 2), BF),
            pltpu.VMEM((Y, X, F, D), BF),
            pltpu.VMEM((R, D, HT), BF),
            pltpu.VMEM((R, HT, D), BF),
            pltpu.VMEM((rows, D), F32),
            pltpu.VMEM((2, D, TILE), BF),
            pltpu.VMEM((2 * DV, F, TILE), BF),
            pltpu.VMEM((T, TILE, TILE), BF),
            pltpu.VMEM((DV, F, TILE), BF),
            pltpu.VMEM((D, TILE), BF),
            pltpu.VMEM((2, Z, 2 * TR, D // 2), BF),
            pltpu.VMEM((Z, 2 * TR, D // 2), BF),
            pltpu.VMEM((Z, 2 * TR, D // 2), BF),
            pltpu.VMEM((Z, 2 * TR, D // 2), BF),
            pltpu.VMEM((2 * TR, D // 2), BF),
            pltpu.VMEM((R, 2 * TR, D // 2), BF),
            pltpu.VMEM((D, TILE), BF),
            pltpu.VMEM((DV, F, TILE), BF),
            pltpu.VMEM((T + 1, F, TILE), F32),
            pltpu.VMEM((2 * DV, F, TILE), BF),
            pltpu.VMEM((2, D, TILE), BF),
            pltpu.VMEM((rows, D), BF),
            pltpu.SemaphoreType.DMA((7,)),
            pltpu.SemaphoreType.DMA((2, DV)),
            pltpu.SemaphoreType.DMA((2,)),
            pltpu.SemaphoreType.DMA((Y,)),
            pltpu.SemaphoreType.DMA((2, 2)),
            pltpu.SemaphoreType.DMA((2,)),
            pltpu.SemaphoreType.DMA((2,)),
            pltpu.SemaphoreType.DMA((2, R)),
            pltpu.SemaphoreType.DMA((2,)),
            pltpu.SemaphoreType.DMA((R,)),
            pltpu.SemaphoreType.DMA((7,)),
            pltpu.SemaphoreType.DMA((7,)),
        ],
        compiler_params=pltpu.CompilerParams(
            collective_id=0, has_side_effects=True, vmem_limit_bytes=60 * 1024 * 1024
        ),
        name="whole_layer",
    )(
        tile_source,
        tile_count,
        tables,
        own_rows,
        rel_w_in[0],
        rel_w_out[0],
        tile_edges[0],
        target_feat,
        norm_gain[None, :],
        tgt_w_in,
        tgt_w_out,
        out_grad,
    )
    return (updated, grad_source[None])


def solution(mesh):
    placed = (
        P("rel", "dev", None),
        P("rel", "dev", None),
        P("rel", "dev", None),
        P("rel", None),
        P("rel", None, None),
        P("rel", None),
        P(("dev", "rel"), None),
        P(),
        P(None, "rel"),
        P("rel", None),
        P(("dev", "rel"), None),
    )
    return jax.shard_map(
        shards,
        mesh=mesh,
        in_specs=placed,
        out_specs=(P(("dev", "rel"), None), P("rel", "dev", None)),
        check_vma=False,
    )
```

```python
import functools

import jax
import jax.numpy as jnp
from jax import lax
from jax.experimental import pallas as pl
from jax.experimental.pallas import tpu as pltpu
from jax.sharding import PartitionSpec as P

TILE = 128
TILE_ROW = 4
RING_X = 4

eps_norm = 1e-06

BF = jnp.bfloat16
F32 = jnp.float32
MESH = pl.DeviceIdType.MESH


def silu_slope(values):
    sigma = jax.nn.sigmoid(values)
    return sigma * (1.0 + values * (1.0 - sigma))


def dot_nn(a, b):
    return lax.dot_general(a, b, (((1,), (0,)), ((), ())), preferred_element_type=F32)


def dot_nt(a, b):
    return lax.dot_general(a, b, (((1,), (1,)), ((), ())), preferred_element_type=F32)


def whole_kernel(
    DV,
    R,
    ids_in,
    live_in,
    src_in,
    win_in,
    wout_in,
    edges_in,
    tfeat_in,
    gain_in,
    twi_in,
    two_in,
    og_in,
    upd_out,
    grad_out,
    ids,
    live,
    ids_v,
    tab_v,
    tab,
    tfeat,
    gain,
    og,
    src,
    edges,
    w_a,
    w_b,
    w_out,
    twi,
    two,
    pre,
    hid_t,
    hid_by_feature,
    counts,
    agg_send,
    agg_recv,
    part_send,
    part_pair,
    part_sum,
    part_recv,
    ga_send,
    ga_recv,
    gt_send,
    gt_recv,
    runs,
    gh_send,
    gh_recv,
    grad_pre,
    copy_sem,
    ring_sem,
    ring_send_sem,
    y_sem,
    x_sem,
    far_sem,
    wout_send_sem,
    z_sem,
    z_send_sem,
    ga_sem,
    send_sem,
    recv_sem,
):
    D = src.shape[1]
    HD = D // 2
    F = D // DV
    T = ids.shape[1]
    TR = tfeat.shape[0]
    X = RING_X
    Y = DV // X
    HY = Y // 2
    Z = R // 2
    HZ = Z // 2
    W = min(256, HD)
    rd = lax.axis_index("rel")
    me = lax.axis_index("dev")
    my_y = me // X
    my_x = lax.rem(me, X)
    my_z = rd // 2
    my_c = lax.rem(rd, 2)

    def take(n, source, place):
        copy = pltpu.make_async_copy(source, place, copy_sem.at[n])
        copy.start()
        return copy

    own_a = take(0, win_in.at[:, pl.ds(0, HD)], w_a.at[me])
    own_b = take(1, win_in.at[:, pl.ds(HD, HD)], w_b.at[me])
    own_twi = take(2, twi_in, twi.at[rd])
    own_two = take(3, two_in, two.at[rd])
    own_out = take(4, wout_in, w_out.at[my_y, my_x])
    own_ids = take(7, ids_in, ids_v)
    own_src = take(5, src_in, src)
    own_edges = take(6, edges_in, edges)
    own_small = [
        take(8, ids_in, ids),
        take(9, live_in, live),
        take(10, tfeat_in, tfeat),
        take(11, gain_in, gain),
        take(12, og_in, og),
    ]

    def col(dx):
        return lax.rem(my_x + dx + X, X)

    def row(dy):
        return lax.rem(my_y + dy + Y, Y)

    def at(dy, dx):
        return row(dy) * X + col(dx)

    def zc(dz, dc=0):
        return lax.rem(my_z + dz + Z, Z) * 2 + lax.rem(my_c + dc, 2)

    barrier = pltpu.get_barrier_semaphore()

    near_dev = (at(1, 0), at(-1, 0), at(0, 1), at(0, -1), at(0, 2))
    near_rel = (zc(1), zc(-1), zc(0, 1))
    for to in near_dev:
        pl.semaphore_signal(barrier, inc=1, device_id={"dev": to}, device_id_type=MESH)
    for to in near_rel:
        pl.semaphore_signal(barrier, inc=1, device_id={"rel": to}, device_id_type=MESH)
    own_a.wait()
    own_b.wait()
    pl.semaphore_wait(barrier, len(near_dev) + len(near_rel))

    def remote(piece, place, sent, got, axis, to):
        pltpu.make_async_remote_copy(
            src_ref=piece,
            dst_ref=place,
            send_sem=sent,
            recv_sem=got,
            device_id={axis: to},
            device_id_type=MESH,
        ).start()

    def all_of(sem, view):
        pltpu.make_async_copy(view, view, sem).wait()

    half = (w_a, w_b)

    def push(h, block, to):
        piece = half[h].at[block]
        remote(piece, piece, ring_send_sem.at[h], ring_sem.at[h, block], "dev", to)

    def arrive(h, block):
        all_of(ring_sem.at[h, block], half[h].at[block])

    def begin_in():
        push(0, me, at(1, 0))
        push(0, me, at(-1, 0))
        push(0, me, at(0, 1))
        push(0, me, at(0, -1))
        push(1, me, at(1, 0))
        push(1, me, at(-1, 0))
        push(0, me, at(0, 2))
        push(1, me, at(0, 1))
        push(1, me, at(0, -1))

    def relay_x(dy):
        even = lax.rem(row(dy), 2) == 0
        arrive(1, at(dy, -1))
        arrive(1, at(dy, 1))
        push(
            1,
            jnp.where(even, at(dy, -1), at(dy, 1)),
            jnp.where(even, at(0, 1), at(0, -1)),
        )

    def first_half(s):
        def column(i, c):
            dx = jnp.where(i == 3, 2, jnp.where(i == 2, 3, i))
            if s == 0:
                arrive(0, at(0, dx))
                push(0, at(0, dx), at(1, 0))
                push(0, at(0, dx), at(-1, 0))
            elif s < HY:
                arrive(0, at(-s, dx))
                if s < HY - 1:
                    push(0, at(-s, dx), at(1, 0))
                arrive(0, at(s, dx))
                if s < HY - 1:
                    push(0, at(s, dx), at(-1, 0))
                else:
                    even = lax.rem(my_x + dx, 2) == 0
                    push(
                        0,
                        jnp.where(even, at(-s, dx), at(s, dx)),
                        jnp.where(even, at(1, 0), at(-1, 0)),
                    )
            else:
                arrive(0, at(HY, dx))
            return c

        lax.fori_loop(1 if s == 0 else 0, X, column, 0)

    def to_row(dy, far):
        push(1, at(dy, 0), at(0, 1))
        push(1, at(dy, 0), at(0, -1))
        if far:
            push(1, at(dy, 0), at(0, 2))

    def second_half(s):
        far = s >= HY - 1
        if 1 <= s < HY:
            for d in (-s, s):
                arrive(1, at(d, 0))
                if s < HY - 1:
                    push(1, at(d, 0), at(1 if d < 0 else -1, 0))
            if s == HY - 1:
                even = lax.rem(my_x, 2) == 0
                push(
                    1,
                    jnp.where(even, at(-s, 0), at(s, 0)),
                    jnp.where(even, at(1, 0), at(-1, 0)),
                )
            for d in (-s, s):
                to_row(d, far)
        elif s == HY:
            arrive(1, at(HY, 0))
            to_row(HY, far)
        if s == 1:
            relay_x(0)
        elif 2 <= s < HY:
            relay_x(-(s - 1))
            relay_x(s - 1)

    def second_rest():
        for d in (-(HY - 1), HY - 1, HY):
            arrive(1, at(d, 1))
            arrive(1, at(d, -1))
        if HY == 2:
            pass

        def rest(i, c):
            arrive(1, i * X + col(2))
            return c

        lax.fori_loop(0, Y, rest, 0)

    def out_push(y, to):
        piece = w_out.at[y, my_x]
        remote(piece, piece, wout_send_sem.at[0], y_sem.at[y], "dev", to)

    def out_arrive(y):
        all_of(y_sem.at[y], w_out.at[y, my_x])

    def out_y(s):
        if s == 0:
            out_push(my_y, at(1, 0))
            out_push(my_y, at(-1, 0))
        elif s < HY:
            out_arrive(row(-s))
            if s < HY - 1:
                out_push(row(-s), at(1, 0))
            out_arrive(row(s))
            if s < HY - 1:
                out_push(row(s), at(-1, 0))
            else:
                even = lax.rem(my_x, 2) == 0
                out_push(
                    jnp.where(even, row(-s), row(s)), jnp.where(even, at(1, 0), at(-1, 0))
                )
        else:
            out_arrive(row(HY))

    def out_x(*rows):
        for dy in rows:
            piece = w_out.at[row(dy), my_x]
            for side in (0, 1):
                to = at(0, 1) if side == 0 else at(0, -1)
                remote(piece, piece, wout_send_sem.at[1], x_sem.at[side, row(dy)], "dev", to)

    def out_relay(*rows):
        for dy in rows:
            y = row(dy)
            even = lax.rem(y, 2) == 0
            all_of(x_sem.at[0, y], w_out.at[y, col(-1)])
            all_of(x_sem.at[1, y], w_out.at[y, col(1)])
            piece = w_out.at[y, jnp.where(even, col(-1), col(1))]
            to = jnp.where(even, at(0, 1), at(0, -1))
            remote(piece, piece, wout_send_sem.at[1], far_sem.at[y], "dev", to)

    def out_far(*rows):
        for dy in rows:
            all_of(far_sem.at[row(dy)], w_out.at[row(dy), col(2)])

    tgt = (twi, two)

    def z_push(w, r, to):
        piece = tgt[w].at[r]
        remote(piece, piece, z_send_sem.at[w], z_sem.at[w, r], "rel", to)

    def z_arrive(w, r):
        all_of(z_sem.at[w, r], tgt[w].at[r])

    def z_step(s, weights=(0, 1)):
        for w in weights:
            if s == 0:
                z_push(w, rd, zc(1))
                z_push(w, rd, zc(-1))
                z_push(w, rd, zc(0, 1))
            elif s < HZ:
                z_arrive(w, zc(-s))
                if s < HZ - 1 or w == 0:
                    z_push(w, zc(-s), zc(1))
                z_arrive(w, zc(s))
                if s < HZ - 1 or w == 1:
                    z_push(w, zc(s), zc(-1))
                z_push(w, zc(-s), zc(0, 1))
                z_push(w, zc(s), zc(0, 1))
            elif s == HZ:
                z_arrive(w, zc(HZ))
                z_push(w, zc(HZ), zc(0, 1))
            else:
                for d in range(Z):
                    z_arrive(w, zc(d, 1))

    def over_dev(n, piece, place):
        def send(i, c):
            m = (i + 1) // 2
            to = lax.rem(me + DV // 2 + jnp.where(lax.rem(i, 2) == 1, m, DV - m), DV)
            remote(piece(to), place, send_sem.at[n], recv_sem.at[n], "dev", to)
            return c

        lax.fori_loop(0, DV - 1, send, 0)

    def folded(rows):
        return jnp.concatenate([rows[..., :HD], rows[..., HD:]], axis=-2).astype(BF)

    def count_tiles(first, number, turned=False):
        lattice = lax.broadcasted_iota(jnp.int32, (TILE, TILE), 0).astype(F32).astype(BF)
        slots = lax.broadcasted_iota(jnp.int32, (1, TILE), 1)
        one = jnp.ones((TILE, TILE), BF)
        none = jnp.zeros((TILE, TILE), BF)

        def hot(spots):
            rows = jnp.broadcast_to(spots.astype(F32), (16, TILE)).astype(BF)
            return jnp.where(lattice == jnp.concatenate([rows] * (TILE // 16), axis=0), one, none)

        def some(i, c):
            for u in range(8):
                k = first + i * 8 + u
                codes = edges[pl.ds(k, 1), :]
                s_at = jnp.bitwise_and(codes, TILE - 1)
                t_at = jnp.where(slots < live[0, k], jnp.right_shift(codes, 7), -1)
                s_hot, t_hot = hot(s_at), hot(t_at)
                pair = (t_hot, s_hot) if turned else (s_hot, t_hot)
                counts[k] = dot_nt(*pair).astype(BF)
            return c

        lax.fori_loop(0, number // 8, some, 0)

    def slice_of(p):
        x = lax.rem(p, X)
        return (x // 2) * (DV // 2) + (p // X) * 2 + lax.rem(x, 2)

    mine = slice_of(me)
    my_rows = pl.ds(pl.multiple_of(mine * F, F), F)

    def rows_for(p):
        return pl.ds(pl.multiple_of(slice_of(p) * F, F), F)

    def first_projection(h):
        def some(j, c):
            cols = pl.ds(pl.multiple_of(j * W, W), W)
            value = dot_nn(src[...], half[h][:, :, cols].reshape(D, W))
            there = pl.ds(pl.multiple_of(h * HD + j * W, W), W)
            pre[:, there] = value
            turned = (value * jax.nn.sigmoid(value)).T.astype(BF)
            hid_t[0, there, :] = turned[:, :TILE]
            hid_t[1, there, :] = turned[:, TILE:]
            return c

        lax.fori_loop(0, HD // W, some, 0)

        def send(i, c):
            dy = i // 2
            to = row(dy) * X + 2 * h + lax.rem(my_x + lax.rem(i, 2), 2)

            @pl.when(to != me)
            def _():
                remote(
                    hid_t.at[:, rows_for(to), :],
                    hid_by_feature.at[pl.ds(2 * me, 2)],
                    send_sem.at[1],
                    recv_sem.at[1],
                    "dev",
                    to,
                )

            return c

        lax.fori_loop(0, DV // 2, send, 0)

    def make_tables():
        spread_ids = jnp.broadcast_to(ids_v[...], (T, T))
        down = spread_ids.T
        ii = lax.broadcasted_iota(jnp.int32, (T, T), 0)
        jj = lax.broadcasted_iota(jnp.int32, (T, T), 1)

        def over_tiles(mask, value):
            return jnp.sum(jnp.where(mask, value, 0), axis=0, keepdims=True)

        earlier = (down < spread_ids) | ((down == spread_ids) & (ii < jj))
        rank = jnp.broadcast_to(over_tiles(earlier, 1), (T, T)).T
        order = over_tiles(rank == jj, ii)
        here = over_tiles(rank == jj, down)
        before = over_tiles(rank + 1 == jj, down + 1) - 1
        upto = over_tiles(down <= jj, 1)
        named = over_tiles(down == jj, 1)
        tab_v[0:1, :] = order
        tab_v[1:2, :] = jnp.right_shift(order, 2)
        tab_v[2:3, :] = jnp.where(here == before, 1, 0)
        tab_v[3:4, :] = jnp.where(named > 0, upto - 1, T)

    begin_in()
    own_twi.wait()
    own_two.wait()
    z_step(0)
    own_ids.wait()
    make_tables()
    own_tab = take(13, tab_v, tab)
    own_out.wait()
    soon = [d for n in range(HY - 1) for d in ((-n, n) if n else (0,))]
    late = [-(HY - 1), HY - 1, HY]
    for s in range(HY + 1):
        first_half(s)
        second_half(s)
        if s == 0:
            out_x(0)
        if s == HY - 2:
            z_step(1, (0,))
            out_y(0)
        if s == HY - 1:
            z_step(1, (1,))
    out_y(1)
    own_src.wait()
    first_projection(0)
    out_x(*soon[1:3])
    second_rest()
    first_projection(1)
    hid_by_feature[pl.ds(2 * me, 2)] = hid_t[:, my_rows, :]
    for s in range(2, HY - 1):
        out_y(s)
        out_x(-s, s)
    out_relay(*soon[:3])
    own_edges.wait()
    for copy in own_small:
        copy.wait()
    own_tab.wait()
    count_tiles(0, T // 2)
    if HZ > 2:
        z_step(2, (0,))
    out_y(HY - 1)
    out_x(-(HY - 1), HY - 1)
    count_tiles(T // 2, T // 2)
    if HZ > 2:
        z_step(2, (1,))
    out_y(HY)
    out_x(HY)
    out_relay(*soon[3:])
    all_of(recv_sem.at[1], hid_by_feature.at[pl.ds(0, 2 * (DV - 1))])

    def aggregate(i, c):
        for u in range(8):
            b = i * 8 + u
            total = jnp.zeros((F, TILE), F32)
            for q in range(TILE_ROW):
                k = b * TILE_ROW + q
                total = total + dot_nn(hid_by_feature[ids[0, k]], counts[k])
            agg_send[b] = total.astype(BF)
        return c

    lax.fori_loop(0, T // TILE_ROW // 8, aggregate, 0)
    over_dev(2, lambda to: agg_send.at[to], agg_recv.at[my_rows])
    agg_recv[my_rows, :] = agg_send[me]
    if HZ > 3:
        z_step(3, (0,))
    out_relay(*late)
    if HZ > 3:
        z_step(3, (1,))
    out_far(*soon)
    out_far(*late)
    z_step(HZ, (0,))
    all_of(recv_sem.at[2], agg_recv.at[pl.ds(0, D - F)])

    agg_hidden = agg_recv[...].astype(F32).T.astype(BF)
    for j in range(HD // W):
        low = dot_nn(agg_hidden, w_out[:, :, :, j * W : (j + 1) * W].reshape(D, W))
        high = dot_nn(agg_hidden, w_out[:, :, :, HD + j * W : HD + (j + 1) * W].reshape(D, W))
        both = jnp.concatenate([low.reshape(R, TR, W), high.reshape(R, TR, W)], axis=1)
        both = both.astype(BF).reshape(Z, 2, 2 * TR, W)
        part_send[0, :, :, j * W : (j + 1) * W] = both[:, 0]
        part_send[1, :, :, j * W : (j + 1) * W] = both[:, 1]
    remote(part_send.at[1 - my_c], part_pair, send_sem.at[0], recv_sem.at[0], "rel", zc(0, 1))

    def wide(rows):
        return (jnp.concatenate([rows, rows], axis=0) if TR < 16 else rows).astype(BF)

    all_of(recv_sem.at[0], part_pair)
    part_sum[...] = (part_send[my_c].astype(F32) + part_pair[...].astype(F32)).astype(BF)
    for d in range(1, Z):
        remote(
            part_sum.at[lax.rem(my_z + d, Z)],
            part_recv.at[my_z],
            send_sem.at[3],
            recv_sem.at[3],
            "rel",
            zc(d),
        )
    part_recv[my_z] = part_sum[my_z]
    z_step(HZ, (1,))
    z_step(HZ + 1)
    og_rows = wide(og[...].astype(F32))
    grad_hidden_t = [dot_nt(og_rows, two[r]) for r in range(R)]
    all_of(recv_sem.at[3], part_recv.at[pl.ds(0, Z - 1)])
    total = part_recv[0].astype(F32)
    for z in range(1, Z):
        total = total + part_recv[z].astype(F32)
    agg = jnp.concatenate([total[:TR], total[TR:]], axis=1)
    gain_row = gain[...]
    inverse_norm = lax.rsqrt(jnp.mean(agg * agg, axis=1, keepdims=True) + eps_norm)
    normed = wide(agg * inverse_norm * gain_row)
    target_pre = [dot_nn(normed, twi[r]) for r in range(R)]
    grad_normed = jnp.zeros((normed.shape[0], D), F32)
    for r in range(R):
        grad_pre_t = (grad_hidden_t[r] * silu_slope(target_pre[r])).astype(BF)
        grad_normed = grad_normed + dot_nt(grad_pre_t, twi[r])
    scaled = grad_normed[:TR] * gain_row
    mean_term = jnp.mean(agg * scaled, axis=1, keepdims=True)
    ga_send[...] = folded(
        inverse_norm * (scaled - agg * inverse_norm * inverse_norm * mean_term)
    )
    for dz in sorted(range(1, Z), key=lambda d: min(d, Z - d)):
        remote(ga_send, ga_recv.at[rd], send_sem.at[4], ga_sem.at[rd], "rel", zc(dz))
    remote(ga_send, ga_recv.at[rd], send_sem.at[4], ga_sem.at[rd], "rel", zc(0, 1))
    ga_recv[rd] = ga_send[...]
    update = jnp.zeros((normed.shape[0], D), F32)
    for r in range(R):
        target_hidden = (target_pre[r] * jax.nn.sigmoid(target_pre[r])).astype(BF)
        update = update + dot_nn(target_hidden, two[r])
    upd_out[...] = (tfeat[...].astype(F32) + update[:TR]).astype(BF)
    for dz in sorted(range(1, Z), key=lambda d: min(d, Z - d)):
        r = zc(dz)
        all_of(ga_sem.at[r], ga_recv.at[r])
        remote(ga_recv.at[r], ga_recv.at[r], send_sem.at[4], ga_sem.at[r], "rel", zc(0, 1))
    for dz in range(Z):
        r = zc(dz, 1)
        all_of(ga_sem.at[r], ga_recv.at[r])

    held = ga_recv[...].astype(F32)
    held = jnp.concatenate([held[:, :TR, :], held[:, TR:, :]], axis=2)
    grad_agg = held.reshape(R * TR, D).astype(BF)
    blocks = W // F
    for j in range(D // W):
        value = dot_nt(grad_agg, w_out[j * blocks // X : (j + 1) * blocks // X].reshape(W, D))
        gt_send[j * W : (j + 1) * W, :] = value.T.astype(BF)
    over_dev(5, lambda to: gt_send.at[rows_for(to)], gt_recv.at[me])
    gt_recv[me] = gt_send[my_rows, :]
    runs[T] = jnp.zeros((F, TILE), F32)
    count_tiles(0, T, True)
    all_of(recv_sem.at[5], gt_recv.at[pl.ds(0, DV - 1)])

    def spread(i, running):
        for u in range(32):
            j = i * 32 + u
            term = dot_nn(gt_recv[tab[1, j]], counts[tab[0, j]])
            running = running * tab[2, j].astype(F32) + term
            runs[j] = running
        return running

    lax.fori_loop(0, T // 32, spread, jnp.zeros((F, TILE), F32))

    def settle(i, c):
        for u in range(8):
            b = i * 8 + u
            gh_send[b] = runs[tab[3, b]].astype(BF)
        return c

    lax.fori_loop(0, 2 * DV // 8, settle, 0)
    over_dev(6, lambda to: gh_send.at[pl.ds(2 * to, 2)], gh_recv.at[:, my_rows, :])
    gh_recv[:, my_rows, :] = gh_send[pl.ds(2 * me, 2)]

    for h in range(2):
        all_of(ring_send_sem.at[h], half[h].at[pl.ds(0, DV - 1)])
        all_of(z_send_sem.at[h], tgt[h].at[pl.ds(0, R - 1)])
    all_of(wout_send_sem.at[0], w_out.at[pl.ds(0, Y - 1), 0])
    all_of(wout_send_sem.at[1], w_out.at[:, pl.ds(0, 3)])
    all_of(send_sem.at[0], part_pair)
    all_of(send_sem.at[1], hid_by_feature.at[pl.ds(0, 2 * (DV - 1))])
    all_of(send_sem.at[2], agg_recv.at[pl.ds(0, D - F)])
    all_of(send_sem.at[3], part_recv.at[pl.ds(0, Z - 1)])
    all_of(send_sem.at[4], ga_recv.at[pl.ds(0, R - 1)])
    all_of(send_sem.at[5], gt_recv.at[pl.ds(0, DV - 1)])

    all_of(recv_sem.at[6], gh_recv.at[:, pl.ds(0, D - F), :])

    def last_slope(j, c):
        cols = pl.ds(pl.multiple_of(j * W, W), W)
        turned = jnp.concatenate([gh_recv[0, cols, :], gh_recv[1, cols, :]], axis=1)
        value = turned.astype(F32).T * silu_slope(pre[:, cols])
        grad_pre[:, cols] = value.astype(BF)
        return c

    lax.fori_loop(0, D // W, last_slope, 0)

    def last_projection(j, c):
        cols = pl.ds(pl.multiple_of(j * W, W), W)
        these = pl.ds(j * blocks, blocks)
        value = dot_nt(grad_pre[:, :HD], w_a[these].reshape(W, HD))
        value = value + dot_nt(grad_pre[:, HD:], w_b[these].reshape(W, HD))
        grad_out[:, cols] = value.astype(BF)
        return c

    lax.fori_loop(0, D // W, last_projection, 0)
    all_of(send_sem.at[6], gh_recv.at[:, pl.ds(0, D - F), :])


def shards(
    src_feat,
    rel_w_in,
    rel_w_out,
    tile_source,
    tile_edges,
    tile_count,
    target_feat,
    norm_gain,
    tgt_w_in,
    tgt_w_out,
    out_grad,
):
    DV = lax.axis_size("dev")
    R = lax.axis_size("rel")
    own_rows = src_feat[0]
    rows, D = own_rows.shape
    F = D // DV
    T = tile_source.shape[1]
    TR = target_feat.shape[0]
    X, Y, Z = RING_X, DV // RING_X, R // 2
    HT = tgt_w_in.shape[1]

    vmem = pl.BlockSpec(memory_space=pltpu.VMEM)
    hbm = pl.BlockSpec(memory_space=pltpu.HBM)
    updated, grad_source = pl.pallas_call(
        functools.partial(whole_kernel, DV, R),
        out_shape=(
            pltpu.VMEM((TR, D), BF),
            pltpu.VMEM((rows, D), BF),
        ),
        in_specs=[hbm] * 11,
        out_specs=(vmem, vmem),
        scratch_shapes=[
            pltpu.SMEM((1, T), jnp.int32),
            pltpu.SMEM((1, T), jnp.int32),
            pltpu.VMEM((1, T), jnp.int32),
            pltpu.VMEM((4, T), jnp.int32),
            pltpu.SMEM((4, T), jnp.int32),
            pltpu.VMEM((TR, D), BF),
            pltpu.VMEM((1, D), F32),
            pltpu.VMEM((TR, D), BF),
            pltpu.VMEM((rows, D), BF),
            pltpu.VMEM((T, TILE), jnp.int32),
            pltpu.VMEM((DV, F, D // 2), BF),
            pltpu.VMEM((DV, F, D // 2), BF),
            pltpu.VMEM((Y, X, F, D), BF),
            pltpu.VMEM((R, D, HT), BF),
            pltpu.VMEM((R, HT, D), BF),
            pltpu.VMEM((rows, D), F32),
            pltpu.VMEM((2, D, TILE), BF),
            pltpu.VMEM((2 * DV, F, TILE), BF),
            pltpu.VMEM((T, TILE, TILE), BF),
            pltpu.VMEM((DV, F, TILE), BF),
            pltpu.VMEM((D, TILE), BF),
            pltpu.VMEM((2, Z, 2 * TR, D // 2), BF),
            pltpu.VMEM((Z, 2 * TR, D // 2), BF),
            pltpu.VMEM((Z, 2 * TR, D // 2), BF),
            pltpu.VMEM((Z, 2 * TR, D // 2), BF),
            pltpu.VMEM((2 * TR, D // 2), BF),
            pltpu.VMEM((R, 2 * TR, D // 2), BF),
            pltpu.VMEM((D, TILE), BF),
            pltpu.VMEM((DV, F, TILE), BF),
            pltpu.VMEM((T + 1, F, TILE), F32),
            pltpu.VMEM((2 * DV, F, TILE), BF),
            pltpu.VMEM((2, D, TILE), BF),
            pltpu.VMEM((rows, D), BF),
            pltpu.SemaphoreType.DMA((14,)),
            pltpu.SemaphoreType.DMA((2, DV)),
            pltpu.SemaphoreType.DMA((2,)),
            pltpu.SemaphoreType.DMA((Y,)),
            pltpu.SemaphoreType.DMA((2, Y)),
            pltpu.SemaphoreType.DMA((Y,)),
            pltpu.SemaphoreType.DMA((2,)),
            pltpu.SemaphoreType.DMA((2, R)),
            pltpu.SemaphoreType.DMA((2,)),
            pltpu.SemaphoreType.DMA((R,)),
            pltpu.SemaphoreType.DMA((7,)),
            pltpu.SemaphoreType.DMA((7,)),
        ],
        compiler_params=pltpu.CompilerParams(
            collective_id=0, has_side_effects=True, vmem_limit_bytes=60 * 1024 * 1024
        ),
        name="whole_layer",
    )(
        tile_source,
        tile_count,
        own_rows,
        rel_w_in[0],
        rel_w_out[0],
        tile_edges[0],
        target_feat,
        norm_gain[None, :],
        tgt_w_in,
        tgt_w_out,
        out_grad,
    )
    return (updated, grad_source[None])


def solution(mesh):
    placed = (
        P("rel", "dev", None),
        P("rel", "dev", None),
        P("rel", "dev", None),
        P("rel", None),
        P("rel", None, None),
        P("rel", None),
        P(("dev", "rel"), None),
        P(),
        P(None, "rel"),
        P("rel", None),
        P(("dev", "rel"), None),
    )
    return jax.shard_map(
        shards,
        mesh=mesh,
        in_specs=placed,
        out_specs=(P(("dev", "rel"), None), P("rel", "dev", None)),
        check_vma=False,
    )
```

```python
import functools

import jax
import jax.numpy as jnp
from jax import lax
from jax.experimental import pallas as pl
from jax.experimental.pallas import tpu as pltpu
from jax.sharding import PartitionSpec as P

TILE = 128
TILE_ROW = 4
RING_X = 4

eps_norm = 1e-06

BF = jnp.bfloat16
F32 = jnp.float32
MESH = pl.DeviceIdType.MESH


def silu_slope(values):
    sigma = jax.nn.sigmoid(values)
    return sigma * (1.0 + values * (1.0 - sigma))


def dot_nn(a, b):
    return lax.dot_general(a, b, (((1,), (0,)), ((), ())), preferred_element_type=F32)


def dot_nt(a, b):
    return lax.dot_general(a, b, (((1,), (1,)), ((), ())), preferred_element_type=F32)


def whole_kernel(
    DV,
    R,
    ids_in,
    live_in,
    src_in,
    win_in,
    wout_in,
    edges_in,
    tfeat_in,
    gain_in,
    twi_in,
    two_in,
    og_in,
    upd_place,
    grad_place,
    ids,
    live,
    ids_v,
    tab_v,
    tab,
    tfeat,
    gain,
    og,
    src,
    edges,
    w_a,
    w_b,
    w_out,
    twi,
    two,
    pre,
    hid_t,
    hid_by_feature,
    counts,
    agg_send,
    agg_recv,
    part_send,
    part_pair,
    part_sum,
    part_recv,
    ga_send,
    ga_recv,
    gt_send,
    gt_recv,
    runs,
    gh_send,
    gh_recv,
    grad_pre,
    upd_out,
    grad_out,
    copy_sem,
    ring_sem,
    ring_send_sem,
    y_sem,
    x_sem,
    far_sem,
    wout_send_sem,
    z_sem,
    z_send_sem,
    ga_sem,
    send_sem,
    recv_sem,
):
    D = src.shape[1]
    HD = D // 2
    F = D // DV
    T = ids.shape[1]
    TR = tfeat.shape[0]
    X = RING_X
    Y = DV // X
    HY = Y // 2
    Z = R // 2
    HZ = Z // 2
    W = min(256, HD)
    rd = lax.axis_index("rel")
    me = lax.axis_index("dev")
    my_y = me // X
    my_x = lax.rem(me, X)
    my_z = rd // 2
    my_c = lax.rem(rd, 2)

    def col(dx):
        return lax.rem(my_x + dx + X, X)

    def row(dy):
        return lax.rem(my_y + dy + Y, Y)

    def at(dy, dx):
        return row(dy) * X + col(dx)

    def zc(dz, dc=0):
        return lax.rem(my_z + dz + Z, Z) * 2 + lax.rem(my_c + dc, 2)

    barrier = pltpu.get_barrier_semaphore()

    near_dev = (at(1, 0), at(-1, 0), at(0, 1), at(0, -1), at(0, 2))
    near_rel = (zc(1), zc(-1), zc(0, 1))
    for to in near_dev:
        pl.semaphore_signal(barrier, inc=1, device_id={"dev": to}, device_id_type=MESH)
    for to in near_rel:
        pl.semaphore_signal(barrier, inc=1, device_id={"rel": to}, device_id_type=MESH)
    def take(n, source, place):
        copy = pltpu.make_async_copy(source, place, copy_sem.at[n])
        copy.start()
        return copy

    own_a = take(0, win_in.at[:, pl.ds(0, HD)], w_a.at[me])
    own_b = take(1, win_in.at[:, pl.ds(HD, HD)], w_b.at[me])
    own_twi = take(2, twi_in, twi.at[rd])
    own_two = take(3, two_in, two.at[rd])
    own_out = take(4, wout_in, w_out.at[my_y, my_x])
    own_ids = take(7, ids_in, ids_v)
    own_src = take(5, src_in, src)
    own_edges = take(6, edges_in, edges)
    own_small = [
        take(8, ids_in, ids),
        take(9, live_in, live),
        take(10, tfeat_in, tfeat),
        take(11, gain_in, gain),
        take(12, og_in, og),
    ]

    own_a.wait()
    own_b.wait()
    pl.semaphore_wait(barrier, len(near_dev) + len(near_rel))

    def remote(piece, place, sent, got, axis, to):
        pltpu.make_async_remote_copy(
            src_ref=piece,
            dst_ref=place,
            send_sem=sent,
            recv_sem=got,
            device_id={axis: to},
            device_id_type=MESH,
        ).start()

    def all_of(sem, view):
        pltpu.make_async_copy(view, view, sem).wait()

    half = (w_a, w_b)

    def push(h, block, to):
        piece = half[h].at[block]
        remote(piece, piece, ring_send_sem.at[h], ring_sem.at[h, block], "dev", to)

    def arrive(h, block):
        all_of(ring_sem.at[h, block], half[h].at[block])

    def begin_in():
        push(0, me, at(1, 0))
        push(0, me, at(-1, 0))
        push(0, me, at(0, 1))
        push(0, me, at(0, -1))
        push(1, me, at(1, 0))
        push(1, me, at(-1, 0))
        push(0, me, at(0, 2))
        push(1, me, at(0, 1))
        push(1, me, at(0, -1))

    def relay_x(dy):
        even = lax.rem(row(dy), 2) == 0
        arrive(1, at(dy, -1))
        arrive(1, at(dy, 1))
        push(
            1,
            jnp.where(even, at(dy, -1), at(dy, 1)),
            jnp.where(even, at(0, 1), at(0, -1)),
        )

    def first_half(s):
        def column(i, c):
            dx = jnp.where(i == 3, 2, jnp.where(i == 2, 3, i))
            if s == 0:
                arrive(0, at(0, dx))
                push(0, at(0, dx), at(1, 0))
                push(0, at(0, dx), at(-1, 0))
            elif s < HY:
                arrive(0, at(-s, dx))
                if s < HY - 1:
                    push(0, at(-s, dx), at(1, 0))
                arrive(0, at(s, dx))
                if s < HY - 1:
                    push(0, at(s, dx), at(-1, 0))
                else:
                    even = lax.rem(my_x + dx, 2) == 0
                    push(
                        0,
                        jnp.where(even, at(-s, dx), at(s, dx)),
                        jnp.where(even, at(1, 0), at(-1, 0)),
                    )
            else:
                arrive(0, at(HY, dx))
            return c

        lax.fori_loop(1 if s == 0 else 0, X, column, 0)

    def to_row(dy, far):
        push(1, at(dy, 0), at(0, 1))
        push(1, at(dy, 0), at(0, -1))
        if far:
            push(1, at(dy, 0), at(0, 2))

    def second_half(s):
        far = s >= HY - 1
        if 1 <= s < HY:
            for d in (-s, s):
                arrive(1, at(d, 0))
                if s < HY - 1:
                    push(1, at(d, 0), at(1 if d < 0 else -1, 0))
            if s == HY - 1:
                even = lax.rem(my_x, 2) == 0
                push(
                    1,
                    jnp.where(even, at(-s, 0), at(s, 0)),
                    jnp.where(even, at(1, 0), at(-1, 0)),
                )
            for d in (-s, s):
                to_row(d, far)
        elif s == HY:
            arrive(1, at(HY, 0))
            to_row(HY, far)
        if s == 1:
            relay_x(0)
        elif 2 <= s < HY:
            relay_x(-(s - 1))
            relay_x(s - 1)

    def second_rest():
        for d in (-(HY - 1), HY - 1, HY):
            arrive(1, at(d, 1))
            arrive(1, at(d, -1))
        if HY == 2:
            pass

        def rest(i, c):
            arrive(1, i * X + col(2))
            return c

        lax.fori_loop(0, Y, rest, 0)

    def out_push(y, to):
        piece = w_out.at[y, my_x]
        remote(piece, piece, wout_send_sem.at[0], y_sem.at[y], "dev", to)

    def out_arrive(y):
        all_of(y_sem.at[y], w_out.at[y, my_x])

    def out_y(s):
        if s == 0:
            out_push(my_y, at(1, 0))
            out_push(my_y, at(-1, 0))
        elif s < HY:
            out_arrive(row(-s))
            if s < HY - 1:
                out_push(row(-s), at(1, 0))
            out_arrive(row(s))
            if s < HY - 1:
                out_push(row(s), at(-1, 0))
            else:
                even = lax.rem(my_x, 2) == 0
                out_push(
                    jnp.where(even, row(-s), row(s)), jnp.where(even, at(1, 0), at(-1, 0))
                )
        else:
            out_arrive(row(HY))

    def out_x(*rows):
        for dy in rows:
            piece = w_out.at[row(dy), my_x]
            for side in (0, 1):
                to = at(0, 1) if side == 0 else at(0, -1)
                remote(piece, piece, wout_send_sem.at[1], x_sem.at[side, row(dy)], "dev", to)

    def out_relay(*rows):
        for dy in rows:
            y = row(dy)
            even = lax.rem(y, 2) == 0
            all_of(x_sem.at[0, y], w_out.at[y, col(-1)])
            all_of(x_sem.at[1, y], w_out.at[y, col(1)])
            piece = w_out.at[y, jnp.where(even, col(-1), col(1))]
            to = jnp.where(even, at(0, 1), at(0, -1))
            remote(piece, piece, wout_send_sem.at[1], far_sem.at[y], "dev", to)

    def out_far(*rows):
        for dy in rows:
            all_of(far_sem.at[row(dy)], w_out.at[row(dy), col(2)])

    tgt = (twi, two)

    def z_push(w, r, to):
        piece = tgt[w].at[r]
        remote(piece, piece, z_send_sem.at[w], z_sem.at[w, r], "rel", to)

    def z_arrive(w, r):
        all_of(z_sem.at[w, r], tgt[w].at[r])

    def z_step(s, weights=(0, 1)):
        for w in weights:
            if s == 0:
                z_push(w, rd, zc(1))
                z_push(w, rd, zc(-1))
                z_push(w, rd, zc(0, 1))
            elif s < HZ:
                z_arrive(w, zc(-s))
                if s < HZ - 1 or w == 0:
                    z_push(w, zc(-s), zc(1))
                z_arrive(w, zc(s))
                if s < HZ - 1 or w == 1:
                    z_push(w, zc(s), zc(-1))
                z_push(w, zc(-s), zc(0, 1))
                z_push(w, zc(s), zc(0, 1))
            elif s == HZ:
                z_arrive(w, zc(HZ))
                z_push(w, zc(HZ), zc(0, 1))
            else:
                for d in range(Z):
                    z_arrive(w, zc(d, 1))

    def wrap(i, n):
        return i - jnp.where(i >= n, n, 0)

    def over_dev(n, piece, place):
        def send(to):
            to = wrap(to, DV)
            remote(piece(to), place, send_sem.at[n], recv_sem.at[n], "dev", to)

        send(me + DV // 2)

        def pair(m, c):
            send(me + DV // 2 - m)
            send(me + DV // 2 + m)
            return c

        lax.fori_loop(1, DV // 2, pair, 0)

    def folded(rows):
        return jnp.concatenate([rows[..., :HD], rows[..., HD:]], axis=-2).astype(BF)

    def count_tiles(first, number, turned=False):
        lattice = lax.broadcasted_iota(jnp.int32, (TILE, TILE), 0).astype(F32).astype(BF)
        slots = lax.broadcasted_iota(jnp.int32, (1, TILE), 1)
        one = jnp.ones((TILE, TILE), BF)
        none = jnp.zeros((TILE, TILE), BF)

        def hot(spots):
            rows = jnp.broadcast_to(spots.astype(F32), (16, TILE)).astype(BF)
            return jnp.where(lattice == jnp.concatenate([rows] * (TILE // 16), axis=0), one, none)

        def some(i, c):
            for u in range(8):
                k = first + i * 8 + u
                codes = edges[pl.ds(k, 1), :]
                s_at = jnp.bitwise_and(codes, TILE - 1)
                t_at = jnp.where(slots < live[0, k], jnp.right_shift(codes, 7), -1)
                s_hot, t_hot = hot(s_at), hot(t_at)
                pair = (t_hot, s_hot) if turned else (s_hot, t_hot)
                counts[k] = dot_nt(*pair).astype(BF)
            return c

        lax.fori_loop(0, number // 8, some, 0)

    def slice_of(p):
        x = lax.rem(p, X)
        return (x // 2) * (DV // 2) + (p // X) * 2 + lax.rem(x, 2)

    mine = slice_of(me)
    my_rows = pl.ds(pl.multiple_of(mine * F, F), F)

    def over_half(h, n, piece, place):
        def send(y, near=False):
            y = wrap(y, Y)
            for bit in range(2):
                to = y * X + 2 * h + bit

                def one(to=to, bit=bit):
                    part = pl.ds(pl.multiple_of((h * (DV // 2) + y * 2 + bit) * F, F), F)
                    remote(piece(part), place, send_sem.at[n], recv_sem.at[n], "dev", to)

                if near:
                    pl.when(to != me)(one)
                else:
                    one()

        send(my_y + HY)

        def pair(m, c):
            send(my_y + HY - m)
            send(my_y + HY + m)
            return c

        lax.fori_loop(1, HY, pair, 0)
        send(my_y, True)

    def first_projection(h):
        def some(j, c):
            cols = pl.ds(pl.multiple_of(j * W, W), W)
            value = dot_nn(src[...], half[h][:, :, cols].reshape(D, W))
            there = pl.ds(pl.multiple_of(h * HD + j * W, W), W)
            pre[:, there] = value
            turned = (value * jax.nn.sigmoid(value)).T.astype(BF)
            hid_t[0, there, :] = turned[:, :TILE]
            hid_t[1, there, :] = turned[:, TILE:]
            return c

        lax.fori_loop(0, HD // W, some, 0)

        over_half(
            h, 1, lambda part: hid_t.at[:, part, :], hid_by_feature.at[pl.ds(2 * me, 2)]
        )

    def make_tables():
        spread_ids = jnp.broadcast_to(ids_v[...], (T, T))
        down = spread_ids.T
        ii = lax.broadcasted_iota(jnp.int32, (T, T), 0)
        jj = lax.broadcasted_iota(jnp.int32, (T, T), 1)

        def over_tiles(mask, value):
            return jnp.sum(jnp.where(mask, value, 0), axis=0, keepdims=True)

        earlier = (down < spread_ids) | ((down == spread_ids) & (ii < jj))
        rank = jnp.broadcast_to(over_tiles(earlier, 1), (T, T)).T
        order = over_tiles(rank == jj, ii)
        here = over_tiles(rank == jj, down)
        before = over_tiles(rank + 1 == jj, down + 1) - 1
        upto = over_tiles(down <= jj, 1)
        named = over_tiles(down == jj, 1)
        tab_v[0:1, :] = order
        tab_v[1:2, :] = jnp.right_shift(order, 2)
        tab_v[2:3, :] = jnp.where(here == before, 1, 0)
        tab_v[3:4, :] = jnp.where(named > 0, upto - 1, T)

    begin_in()
    own_twi.wait()
    own_two.wait()
    z_step(0)
    own_ids.wait()
    make_tables()
    own_tab = take(13, tab_v, tab)
    own_out.wait()
    soon = [d for n in range(HY - 1) for d in ((-n, n) if n else (0,))]
    late = [-(HY - 1), HY - 1, HY]
    for s in range(HY + 1):
        first_half(s)
        second_half(s)
        if s == 0:
            out_x(0)
        if s == HY - 3:
            out_y(0)
        if s == HY - 2:
            z_step(1, (0,))
        if s == HY - 1:
            z_step(1, (1,))
            out_y(1)
            out_x(*soon[1:3])
    for s in range(2, HY - 1):
        out_y(s)
    own_src.wait()
    first_projection(0)
    out_x(*soon[3:])
    own_edges.wait()
    for copy in own_small:
        copy.wait()
    own_tab.wait()
    count_tiles(0, T // 2)
    second_rest()
    out_y(HY - 1)
    first_projection(1)
    hid_by_feature[pl.ds(2 * me, 2)] = hid_t[:, my_rows, :]
    out_x(-(HY - 1), HY - 1)
    if HZ > 2:
        z_step(2, (0,))
    out_y(HY)
    out_x(HY)
    out_relay(*soon[:3])
    count_tiles(T // 2, T // 2)
    if HZ > 2:
        z_step(2, (1,))
    all_of(recv_sem.at[1], hid_by_feature.at[pl.ds(0, 2 * (DV - 1))])

    def sum_block(b):
        total = jnp.zeros((F, TILE), F32)
        for q in range(TILE_ROW):
            k = b * TILE_ROW + q
            total = total + dot_nn(hid_by_feature[ids[0, k]], counts[k])
        agg_send[b] = total.astype(BF)

    def send_block(b):
        remote(agg_send.at[b], agg_recv.at[my_rows], send_sem.at[2], recv_sem.at[2], "dev", b)

    def aggregate(i, c):
        near = [i * 4 + u for u in range(4)]
        pairs = [
            (wrap(me + DV // 2 - m, DV), wrap(me + DV // 2 + 1 + m, DV)) for m in near
        ]
        for pair in pairs:
            for b in pair:
                sum_block(b)
        for low, high in pairs:
            send_block(low)
            pl.when(high != me)(lambda high=high: send_block(high))
        return c

    lax.fori_loop(0, DV // 8, aggregate, 0)
    agg_recv[my_rows, :] = agg_send[me]
    out_relay(*soon[3:])
    out_relay(*late)
    if HZ > 3:
        z_step(3)
    out_far(*soon)
    out_far(*late)
    all_of(recv_sem.at[2], agg_recv.at[pl.ds(0, D - F)])

    agg_hidden = agg_recv[...].astype(F32).T.astype(BF)
    for j in range(HD // W):
        low = dot_nn(agg_hidden, w_out[:, :, :, j * W : (j + 1) * W].reshape(D, W))
        high = dot_nn(agg_hidden, w_out[:, :, :, HD + j * W : HD + (j + 1) * W].reshape(D, W))
        both = jnp.concatenate([low.reshape(R, TR, W), high.reshape(R, TR, W)], axis=1)
        both = both.astype(BF).reshape(Z, 2, 2 * TR, W)
        part_send[0, :, :, j * W : (j + 1) * W] = both[:, 0]
        part_send[1, :, :, j * W : (j + 1) * W] = both[:, 1]
    remote(part_send.at[1 - my_c], part_pair, send_sem.at[0], recv_sem.at[0], "rel", zc(0, 1))

    def wide(rows):
        return (jnp.concatenate([rows, rows], axis=0) if TR < 16 else rows).astype(BF)

    all_of(recv_sem.at[0], part_pair)
    part_sum[...] = (part_send[my_c].astype(F32) + part_pair[...].astype(F32)).astype(BF)
    for d in sorted(range(1, Z), key=lambda d: -min(d, Z - d)):
        remote(
            part_sum.at[lax.rem(my_z + d, Z)],
            part_recv.at[my_z],
            send_sem.at[3],
            recv_sem.at[3],
            "rel",
            zc(d),
        )
    part_recv[my_z] = part_sum[my_z]
    z_step(HZ)
    z_step(HZ + 1)
    og_rows = wide(og[...].astype(F32))
    grad_hidden_t = [dot_nt(og_rows, two[r]) for r in range(R)]
    all_of(recv_sem.at[3], part_recv.at[pl.ds(0, Z - 1)])
    total = part_recv[0].astype(F32)
    for z in range(1, Z):
        total = total + part_recv[z].astype(F32)
    agg = jnp.concatenate([total[:TR], total[TR:]], axis=1)
    gain_row = gain[...]
    inverse_norm = lax.rsqrt(jnp.mean(agg * agg, axis=1, keepdims=True) + eps_norm)
    normed = wide(agg * inverse_norm * gain_row)
    target_pre = [dot_nn(normed, twi[r]) for r in range(R)]
    grad_normed = jnp.zeros((normed.shape[0], D), F32)
    for r in range(R):
        grad_pre_t = (grad_hidden_t[r] * silu_slope(target_pre[r])).astype(BF)
        grad_normed = grad_normed + dot_nt(grad_pre_t, twi[r])
    scaled = grad_normed[:TR] * gain_row
    mean_term = jnp.mean(agg * scaled, axis=1, keepdims=True)
    ga_send[...] = folded(
        inverse_norm * (scaled - agg * inverse_norm * inverse_norm * mean_term)
    )
    for dz in sorted(range(1, Z), key=lambda d: -min(d, Z - d)):
        remote(ga_send, ga_recv.at[rd], send_sem.at[4], ga_sem.at[rd], "rel", zc(dz))
    remote(ga_send, ga_recv.at[rd], send_sem.at[4], ga_sem.at[rd], "rel", zc(0, 1))
    ga_recv[rd] = ga_send[...]
    update = jnp.zeros((normed.shape[0], D), F32)
    for r in range(R):
        target_hidden = (target_pre[r] * jax.nn.sigmoid(target_pre[r])).astype(BF)
        update = update + dot_nn(target_hidden, two[r])
    upd_out[...] = (tfeat[...].astype(F32) + update[:TR]).astype(BF)
    put_upd = take(14, upd_out, upd_place)
    for dz in sorted(range(1, Z), key=lambda d: min(d, Z - d)):
        r = zc(dz)
        all_of(ga_sem.at[r], ga_recv.at[r])
        remote(ga_recv.at[r], ga_recv.at[r], send_sem.at[4], ga_sem.at[r], "rel", zc(0, 1))
    for dz in range(Z):
        r = zc(dz, 1)
        all_of(ga_sem.at[r], ga_recv.at[r])

    held = ga_recv[...].astype(F32)
    held = jnp.concatenate([held[:, :TR, :], held[:, TR:, :]], axis=2)
    grad_agg = held.reshape(R * TR, D).astype(BF)
    blocks = W // F
    for j in range(D // W):
        value = dot_nt(grad_agg, w_out[j * blocks // X : (j + 1) * blocks // X].reshape(W, D))
        gt_send[j * W : (j + 1) * W, :] = value.T.astype(BF)
        if (j + 1) * W % HD == 0:
            half_done = (j + 1) * W // HD - 1
            over_half(half_done, 5, lambda part: gt_send.at[part], gt_recv.at[me])
    gt_recv[me] = gt_send[my_rows, :]
    runs[T] = jnp.zeros((F, TILE), F32)
    count_tiles(0, T, True)
    all_of(recv_sem.at[5], gt_recv.at[pl.ds(0, DV - 1)])

    def spread(i, running):
        for u in range(32):
            j = i * 32 + u
            term = dot_nn(gt_recv[tab[1, j]], counts[tab[0, j]])
            running = running * tab[2, j].astype(F32) + term
            runs[j] = running
        return running

    lax.fori_loop(0, T // 32, spread, jnp.zeros((F, TILE), F32))

    def settle(i, c):
        for u in range(8):
            b = i * 8 + u
            gh_send[b] = runs[tab[3, b]].astype(BF)
        return c

    lax.fori_loop(0, 2 * DV // 8, settle, 0)
    for h in range(2):
        over_dev(6 + h, lambda to: gh_send.at[2 * to + h], gh_recv.at[h, my_rows, :])
    gh_recv[:, my_rows, :] = gh_send[pl.ds(2 * me, 2)]

    for h in range(2):
        all_of(ring_send_sem.at[h], half[h].at[pl.ds(0, DV - 1)])
        all_of(z_send_sem.at[h], tgt[h].at[pl.ds(0, R - 1)])
    all_of(wout_send_sem.at[0], w_out.at[pl.ds(0, Y - 1), 0])
    all_of(wout_send_sem.at[1], w_out.at[:, pl.ds(0, 3)])
    all_of(send_sem.at[0], part_pair)
    all_of(send_sem.at[1], hid_by_feature.at[pl.ds(0, 2 * (DV - 1))])
    all_of(send_sem.at[2], agg_recv.at[pl.ds(0, D - F)])
    all_of(send_sem.at[3], part_recv.at[pl.ds(0, Z - 1)])
    all_of(send_sem.at[4], ga_recv.at[pl.ds(0, R - 1)])
    all_of(send_sem.at[5], gt_recv.at[pl.ds(0, DV - 1)])

    def put_grad(h, j):
        part = (pl.ds(h * TILE, TILE), pl.ds(pl.multiple_of(j * W, W), W))
        return pltpu.make_async_copy(
            grad_out.at[part], grad_place.at[part], copy_sem.at[15 + h * (D // W) + j]
        )

    def slopes(j, c):
        cols = pl.ds(pl.multiple_of(j * W, W), W)
        pre[:, cols] = silu_slope(pre[:, cols])
        return c

    lax.fori_loop(0, D // W, slopes, 0)

    for h in range(2):
        these_rows = slice(h * TILE, (h + 1) * TILE)
        all_of(recv_sem.at[6 + h], gh_recv.at[h, pl.ds(0, D - F), :])

        def last_slope(j, c):
            cols = pl.ds(pl.multiple_of(j * W, W), W)
            value = gh_recv[h, cols, :].astype(F32).T * pre[these_rows, cols]
            grad_pre[these_rows, cols] = value.astype(BF)
            return c

        lax.fori_loop(0, D // W, last_slope, 0)

        def last_projection(j, c):
            cols = pl.ds(pl.multiple_of(j * W, W), W)
            these = pl.ds(j * blocks, blocks)
            value = dot_nt(grad_pre[these_rows, :HD], w_a[these].reshape(W, HD))
            value = value + dot_nt(grad_pre[these_rows, HD:], w_b[these].reshape(W, HD))
            grad_out[these_rows, cols] = value.astype(BF)
            put_grad(h, j).start()
            return c

        lax.fori_loop(0, D // W, last_projection, 0)
    put_upd.wait()
    for h in range(2):
        for j in range(D // W):
            put_grad(h, j).wait()
    for h in range(2):
        all_of(send_sem.at[6 + h], gh_recv.at[h, pl.ds(0, D - F), :])


def shards(
    src_feat,
    rel_w_in,
    rel_w_out,
    tile_source,
    tile_edges,
    tile_count,
    target_feat,
    norm_gain,
    tgt_w_in,
    tgt_w_out,
    out_grad,
):
    DV = lax.axis_size("dev")
    R = lax.axis_size("rel")
    own_rows = src_feat[0]
    rows, D = own_rows.shape
    F = D // DV
    T = tile_source.shape[1]
    TR = target_feat.shape[0]
    X, Y, Z = RING_X, DV // RING_X, R // 2
    HT = tgt_w_in.shape[1]

    place = pl.BlockSpec(memory_space=pl.ANY)
    W = min(256, D // 2)
    hbm = pl.BlockSpec(memory_space=pltpu.HBM)
    updated, grad_source = pl.pallas_call(
        functools.partial(whole_kernel, DV, R),
        out_shape=(
            pltpu.VMEM((TR, D), BF),
            pltpu.VMEM((rows, D), BF),
        ),
        in_specs=[hbm] * 11,
        out_specs=(place, place),
        scratch_shapes=[
            pltpu.SMEM((1, T), jnp.int32),
            pltpu.SMEM((1, T), jnp.int32),
            pltpu.VMEM((1, T), jnp.int32),
            pltpu.VMEM((4, T), jnp.int32),
            pltpu.SMEM((4, T), jnp.int32),
            pltpu.VMEM((TR, D), BF),
            pltpu.VMEM((1, D), F32),
            pltpu.VMEM((TR, D), BF),
            pltpu.VMEM((rows, D), BF),
            pltpu.VMEM((T, TILE), jnp.int32),
            pltpu.VMEM((DV, F, D // 2), BF),
            pltpu.VMEM((DV, F, D // 2), BF),
            pltpu.VMEM((Y, X, F, D), BF),
            pltpu.VMEM((R, D, HT), BF),
            pltpu.VMEM((R, HT, D), BF),
            pltpu.VMEM((rows, D), F32),
            pltpu.VMEM((2, D, TILE), BF),
            pltpu.VMEM((2 * DV, F, TILE), BF),
            pltpu.VMEM((T, TILE, TILE), BF),
            pltpu.VMEM((DV, F, TILE), BF),
            pltpu.VMEM((D, TILE), BF),
            pltpu.VMEM((2, Z, 2 * TR, D // 2), BF),
            pltpu.VMEM((Z, 2 * TR, D // 2), BF),
            pltpu.VMEM((Z, 2 * TR, D // 2), BF),
            pltpu.VMEM((Z, 2 * TR, D // 2), BF),
            pltpu.VMEM((2 * TR, D // 2), BF),
            pltpu.VMEM((R, 2 * TR, D // 2), BF),
            pltpu.VMEM((D, TILE), BF),
            pltpu.VMEM((DV, F, TILE), BF),
            pltpu.VMEM((T + 1, F, TILE), F32),
            pltpu.VMEM((2 * DV, F, TILE), BF),
            pltpu.VMEM((2, D, TILE), BF),
            pltpu.VMEM((rows, D), BF),
            pltpu.VMEM((TR, D), BF),
            pltpu.VMEM((rows, D), BF),
            pltpu.SemaphoreType.DMA((15 + 2 * D // W,)),
            pltpu.SemaphoreType.DMA((2, DV)),
            pltpu.SemaphoreType.DMA((2,)),
            pltpu.SemaphoreType.DMA((Y,)),
            pltpu.SemaphoreType.DMA((2, Y)),
            pltpu.SemaphoreType.DMA((Y,)),
            pltpu.SemaphoreType.DMA((2,)),
            pltpu.SemaphoreType.DMA((2, R)),
            pltpu.SemaphoreType.DMA((2,)),
            pltpu.SemaphoreType.DMA((R,)),
            pltpu.SemaphoreType.DMA((8,)),
            pltpu.SemaphoreType.DMA((8,)),
        ],
        compiler_params=pltpu.CompilerParams(
            collective_id=0, has_side_effects=True, vmem_limit_bytes=60 * 1024 * 1024
        ),
        name="whole_layer",
    )(
        tile_source,
        tile_count,
        own_rows,
        rel_w_in[0],
        rel_w_out[0],
        tile_edges[0],
        target_feat,
        norm_gain[None, :],
        tgt_w_in,
        tgt_w_out,
        out_grad,
    )
    return (updated, grad_source[None])


def solution(mesh):
    placed = (
        P("rel", "dev", None),
        P("rel", "dev", None),
        P("rel", "dev", None),
        P("rel", None),
        P("rel", None, None),
        P("rel", None),
        P(("dev", "rel"), None),
        P(),
        P(None, "rel"),
        P("rel", None),
        P(("dev", "rel"), None),
    )
    return jax.shard_map(
        shards,
        mesh=mesh,
        in_specs=placed,
        out_specs=(P(("dev", "rel"), None), P("rel", "dev", None)),
        check_vma=False,
    )
```

```python
import functools

import jax
import jax.numpy as jnp
from jax import lax
from jax.experimental import pallas as pl
from jax.experimental.pallas import tpu as pltpu
from jax.sharding import PartitionSpec as P

TILE = 128
TILE_ROW = 4
RING_X = 4

eps_norm = 1e-06

BF = jnp.bfloat16
F32 = jnp.float32
MESH = pl.DeviceIdType.MESH


def silu_slope(values):
    sigma = jax.nn.sigmoid(values)
    return sigma * (1.0 + values * (1.0 - sigma))


def dot_nn(a, b):
    return lax.dot_general(a, b, (((1,), (0,)), ((), ())), preferred_element_type=F32)


def dot_nt(a, b):
    return lax.dot_general(a, b, (((1,), (1,)), ((), ())), preferred_element_type=F32)


def whole_kernel(
    DV,
    R,
    ids_in,
    live_in,
    src_in,
    win_in,
    wout_in,
    edges_in,
    tfeat_in,
    gain_in,
    twi_in,
    two_in,
    og_in,
    upd_place,
    grad_place,
    ids,
    live,
    ids_v,
    tab_v,
    tab,
    tfeat,
    gain,
    og,
    src,
    edges,
    w_a,
    w_b,
    w_out,
    twi,
    two,
    pre,
    hid_t,
    hid_by_feature,
    counts,
    agg_send,
    agg_recv,
    part_send,
    part_pair,
    part_sum,
    part_recv,
    ga_send,
    ga_recv,
    gt_send,
    gt_recv,
    runs,
    gh_send,
    gh_recv,
    grad_pre,
    upd_out,
    grad_out,
    copy_sem,
    ring_sem,
    ring_send_sem,
    y_sem,
    x_sem,
    far_sem,
    wout_send_sem,
    z_sem,
    z_pair_sem,
    z_send_sem,
    ga_sem,
    ga_pair_sem,
    send_sem,
    recv_sem,
):
    D = src.shape[1]
    HD = D // 2
    F = D // DV
    T = ids.shape[1]
    TR = tfeat.shape[0]
    X = RING_X
    Y = DV // X
    HY = Y // 2
    Z = R // 2
    HZ = Z // 2
    W = min(256, HD)
    rd = lax.axis_index("rel")
    me = lax.axis_index("dev")
    my_y = me // X
    my_x = lax.rem(me, X)
    my_z = rd // 2
    my_c = lax.rem(rd, 2)

    def col(dx):
        return lax.rem(my_x + dx + X, X)

    def row(dy):
        return lax.rem(my_y + dy + Y, Y)

    def at(dy, dx):
        return row(dy) * X + col(dx)

    def zc(dz, dc=0):
        return lax.rem(my_z + dz + Z, Z) * 2 + lax.rem(my_c + dc, 2)

    barrier = pltpu.get_barrier_semaphore()

    near_dev = (at(1, 0), at(-1, 0), at(0, 1), at(0, -1), at(0, 2))
    near_rel = (zc(1), zc(-1), zc(0, 1))
    for to in near_dev:
        pl.semaphore_signal(barrier, inc=1, device_id={"dev": to}, device_id_type=MESH)
    for to in near_rel:
        pl.semaphore_signal(barrier, inc=1, device_id={"rel": to}, device_id_type=MESH)
    def take(n, source, place):
        copy = pltpu.make_async_copy(source, place, copy_sem.at[n])
        copy.start()
        return copy

    own_a = take(0, win_in.at[:, pl.ds(0, HD)], w_a.at[me])
    own_b = take(1, win_in.at[:, pl.ds(HD, HD)], w_b.at[me])
    own_twi = take(2, twi_in, twi.at[rd])
    own_two = take(3, two_in, two.at[rd])
    own_out = take(4, wout_in, w_out.at[my_y, my_x])
    own_ids = take(7, ids_in, ids_v)
    own_src = take(5, src_in, src)
    own_edges = take(6, edges_in, edges)
    own_small = [
        take(8, ids_in, ids),
        take(9, live_in, live),
        take(10, tfeat_in, tfeat),
        take(11, gain_in, gain),
        take(12, og_in, og),
    ]

    own_a.wait()
    own_b.wait()
    pl.semaphore_wait(barrier, len(near_dev) + len(near_rel))

    def remote(piece, place, sent, got, axis, to):
        pltpu.make_async_remote_copy(
            src_ref=piece,
            dst_ref=place,
            send_sem=sent,
            recv_sem=got,
            device_id={axis: to},
            device_id_type=MESH,
        ).start()

    def all_of(sem, view):
        pltpu.make_async_copy(view, view, sem).wait()

    half = (w_a, w_b)

    def push(h, block, to):
        piece = half[h].at[block]
        remote(piece, piece, ring_send_sem.at[h], ring_sem.at[h, block], "dev", to)

    def arrive(h, block):
        all_of(ring_sem.at[h, block], half[h].at[block])

    def begin_in():
        push(0, me, at(1, 0))
        push(0, me, at(-1, 0))
        push(0, me, at(0, 1))
        push(0, me, at(0, -1))
        push(1, me, at(1, 0))
        push(1, me, at(-1, 0))
        push(0, me, at(0, 2))
        push(1, me, at(0, 1))
        push(1, me, at(0, -1))

    def relay_x(dy):
        even = lax.rem(row(dy), 2) == 0
        arrive(1, at(dy, -1))
        arrive(1, at(dy, 1))
        push(
            1,
            jnp.where(even, at(dy, -1), at(dy, 1)),
            jnp.where(even, at(0, 1), at(0, -1)),
        )

    def first_half(s):
        def column(i, c):
            dx = jnp.where(i == 3, 2, jnp.where(i == 2, 3, i))
            if s == 0:
                arrive(0, at(0, dx))
                push(0, at(0, dx), at(1, 0))
                push(0, at(0, dx), at(-1, 0))
            elif s < HY:
                arrive(0, at(-s, dx))
                if s < HY - 1:
                    push(0, at(-s, dx), at(1, 0))
                arrive(0, at(s, dx))
                if s < HY - 1:
                    push(0, at(s, dx), at(-1, 0))
                else:
                    even = lax.rem(my_x + dx, 2) == 0
                    push(
                        0,
                        jnp.where(even, at(-s, dx), at(s, dx)),
                        jnp.where(even, at(1, 0), at(-1, 0)),
                    )
            else:
                arrive(0, at(HY, dx))
            return c

        lax.fori_loop(1 if s == 0 else 0, X, column, 0)

    def to_row(dy, far):
        push(1, at(dy, 0), at(0, 1))
        push(1, at(dy, 0), at(0, -1))
        if far:
            push(1, at(dy, 0), at(0, 2))

    def second_half(s):
        far = s >= HY - 1
        if 1 <= s < HY:
            for d in (-s, s):
                arrive(1, at(d, 0))
                if s < HY - 1:
                    push(1, at(d, 0), at(1 if d < 0 else -1, 0))
            if s == HY - 1:
                even = lax.rem(my_x, 2) == 0
                push(
                    1,
                    jnp.where(even, at(-s, 0), at(s, 0)),
                    jnp.where(even, at(1, 0), at(-1, 0)),
                )
            for d in (-s, s):
                to_row(d, far)
        elif s == HY:
            arrive(1, at(HY, 0))
            to_row(HY, far)
        if s == 1:
            relay_x(0)
        elif 2 <= s < HY:
            relay_x(-(s - 1))
            relay_x(s - 1)

    def second_rest():
        for d in (-(HY - 1), HY - 1, HY):
            arrive(1, at(d, 1))
            arrive(1, at(d, -1))
        if HY == 2:
            pass

        def rest(i, c):
            arrive(1, i * X + col(2))
            return c

        lax.fori_loop(0, Y, rest, 0)

    def out_push(y, to):
        piece = w_out.at[y, my_x]
        remote(piece, piece, wout_send_sem.at[0], y_sem.at[y], "dev", to)

    def out_arrive(y):
        all_of(y_sem.at[y], w_out.at[y, my_x])

    def out_y(s):
        if s == 0:
            out_push(my_y, at(1, 0))
            out_push(my_y, at(-1, 0))
        elif s < HY:
            out_arrive(row(-s))
            if s < HY - 1:
                out_push(row(-s), at(1, 0))
            out_arrive(row(s))
            if s < HY - 1:
                out_push(row(s), at(-1, 0))
            else:
                even = lax.rem(my_x, 2) == 0
                out_push(
                    jnp.where(even, row(-s), row(s)), jnp.where(even, at(1, 0), at(-1, 0))
                )
        else:
            out_arrive(row(HY))

    def out_x(*rows):
        for dy in rows:
            piece = w_out.at[row(dy), my_x]
            for side in (0, 1):
                to = at(0, 1) if side == 0 else at(0, -1)
                remote(piece, piece, wout_send_sem.at[1], x_sem.at[side, row(dy)], "dev", to)

    def out_relay(*rows):
        for dy in rows:
            y = row(dy)
            even = lax.rem(y, 2) == 0
            all_of(x_sem.at[0, y], w_out.at[y, col(-1)])
            all_of(x_sem.at[1, y], w_out.at[y, col(1)])
            piece = w_out.at[y, jnp.where(even, col(-1), col(1))]
            to = jnp.where(even, at(0, 1), at(0, -1))
            remote(piece, piece, wout_send_sem.at[1], far_sem.at[0], "dev", to)

    def out_far():
        all_of(far_sem.at[0], w_out.at[:, col(2)])

    tgt = (twi, two)

    def z_push(w, r, to):
        piece = tgt[w].at[r]
        remote(piece, piece, z_send_sem.at[w], z_sem.at[w, lax.div(r, 2)], "rel", to)

    def z_pair(w, r):
        piece = tgt[w].at[r]
        remote(piece, piece, z_send_sem.at[w], z_pair_sem.at[w], "rel", zc(0, 1))

    def z_arrive(w, r):
        all_of(z_sem.at[w, lax.div(r, 2)], tgt[w].at[r])

    def z_step(s, weights=(0, 1)):
        for w in weights:
            if s == 0:
                z_push(w, rd, zc(1))
                z_push(w, rd, zc(-1))
                z_pair(w, rd)
            elif s < HZ:
                z_arrive(w, zc(-s))
                if s < HZ - 1 or w == 0:
                    z_push(w, zc(-s), zc(1))
                z_arrive(w, zc(s))
                if s < HZ - 1 or w == 1:
                    z_push(w, zc(s), zc(-1))
                z_pair(w, zc(-s))
                z_pair(w, zc(s))
            elif s == HZ:
                z_arrive(w, zc(HZ))
                z_pair(w, zc(HZ))
            else:
                all_of(z_pair_sem.at[w], tgt[w].at[pl.ds(0, Z)])

    def wrap(i, n):
        return i - jnp.where(i >= n, n, 0)

    def over_dev(n, piece, place):
        def send(to):
            to = wrap(to, DV)
            remote(piece(to), place, send_sem.at[n], recv_sem.at[n], "dev", to)

        send(me + DV // 2)

        def pair(m, c):
            send(me + DV // 2 - m)
            send(me + DV // 2 + m)
            return c

        lax.fori_loop(1, DV // 2, pair, 0)

    def folded(rows):
        return jnp.concatenate([rows[..., :HD], rows[..., HD:]], axis=-2).astype(BF)

    def count_tiles(first, number, turned=False):
        lattice = lax.broadcasted_iota(jnp.int32, (TILE, TILE), 0).astype(F32).astype(BF)
        slots = lax.broadcasted_iota(jnp.int32, (1, TILE), 1)
        one = jnp.ones((TILE, TILE), BF)
        none = jnp.zeros((TILE, TILE), BF)

        def hot(spots):
            rows = jnp.broadcast_to(spots.astype(F32), (16, TILE)).astype(BF)
            return jnp.where(lattice == jnp.concatenate([rows] * (TILE // 16), axis=0), one, none)

        def some(i, c):
            for u in range(8):
                k = first + i * 8 + u
                codes = edges[pl.ds(k, 1), :]
                s_at = jnp.bitwise_and(codes, TILE - 1)
                t_at = jnp.where(slots < live[0, k], jnp.right_shift(codes, 7), -1)
                s_hot, t_hot = hot(s_at), hot(t_at)
                pair = (t_hot, s_hot) if turned else (s_hot, t_hot)
                counts[k] = dot_nt(*pair).astype(BF)
            return c

        lax.fori_loop(0, number // 8, some, 0)

    def slice_of(p):
        x = lax.rem(p, X)
        return (x // 2) * (DV // 2) + (p // X) * 2 + lax.rem(x, 2)

    mine = slice_of(me)
    my_rows = pl.ds(pl.multiple_of(mine * F, F), F)

    def over_half(h, n, piece, place):
        def send(y, near=False):
            y = wrap(y, Y)
            for bit in range(2):
                to = y * X + 2 * h + bit

                def one(to=to, bit=bit):
                    part = pl.ds(pl.multiple_of((h * (DV // 2) + y * 2 + bit) * F, F), F)
                    remote(piece(part), place, send_sem.at[n], recv_sem.at[n], "dev", to)

                if near:
                    pl.when(to != me)(one)
                else:
                    one()

        send(my_y + HY)

        def pair(m, c):
            send(my_y + HY - m)
            send(my_y + HY + m)
            return c

        lax.fori_loop(1, HY, pair, 0)
        send(my_y, True)

    def first_projection(h):
        def some(j, c):
            cols = pl.ds(pl.multiple_of(j * W, W), W)
            value = dot_nn(src[...], half[h][:, :, cols].reshape(D, W))
            there = pl.ds(pl.multiple_of(h * HD + j * W, W), W)
            pre[:, there] = value
            turned = (value * jax.nn.sigmoid(value)).T.astype(BF)
            hid_t[0, there, :] = turned[:, :TILE]
            hid_t[1, there, :] = turned[:, TILE:]
            return c

        lax.fori_loop(0, HD // W, some, 0)

        over_half(
            h, 1, lambda part: hid_t.at[:, part, :], hid_by_feature.at[pl.ds(2 * me, 2)]
        )

    def make_tables():
        spread_ids = jnp.broadcast_to(ids_v[...], (T, T))
        down = spread_ids.T
        ii = lax.broadcasted_iota(jnp.int32, (T, T), 0)
        jj = lax.broadcasted_iota(jnp.int32, (T, T), 1)

        def over_tiles(mask, value):
            return jnp.sum(jnp.where(mask, value, 0), axis=0, keepdims=True)

        earlier = (down < spread_ids) | ((down == spread_ids) & (ii < jj))
        rank = jnp.broadcast_to(over_tiles(earlier, 1), (T, T)).T
        order = over_tiles(rank == jj, ii)
        here = over_tiles(rank == jj, down)
        before = over_tiles(rank + 1 == jj, down + 1) - 1
        upto = over_tiles(down <= jj, 1)
        named = over_tiles(down == jj, 1)
        tab_v[0:1, :] = order
        tab_v[1:2, :] = jnp.right_shift(order, 2)
        tab_v[2:3, :] = jnp.where(here == before, 1, 0)
        tab_v[3:4, :] = jnp.where(named > 0, upto - 1, T)

    begin_in()
    own_twi.wait()
    own_two.wait()
    z_step(0)
    own_ids.wait()
    make_tables()
    own_tab = take(13, tab_v, tab)
    own_out.wait()
    soon = [d for n in range(HY - 1) for d in ((-n, n) if n else (0,))]
    late = [-(HY - 1), HY - 1, HY]
    for s in range(HY + 1):
        first_half(s)
        second_half(s)
        if s == 0:
            out_x(0)
        if s == HY - 3:
            out_y(0)
        if s == HY - 2:
            z_step(1, (0,))
        if s == HY - 1:
            z_step(1, (1,))
            out_y(1)
            out_x(*soon[1:3])
    for s in range(2, HY - 1):
        out_y(s)
    own_src.wait()
    first_projection(0)
    own_edges.wait()
    for copy in own_small:
        copy.wait()
    own_tab.wait()
    count_tiles(0, T // 2)
    out_y(HY - 1)
    second_rest()
    first_projection(1)
    hid_by_feature[pl.ds(2 * me, 2)] = hid_t[:, my_rows, :]
    out_x(*soon[3:])
    out_x(-(HY - 1), HY - 1)
    if HZ > 2:
        z_step(2, (0,))
    out_y(HY)
    out_x(HY)
    out_relay(*soon[:3])
    if HZ > 2:
        z_step(2, (1,))
    count_tiles(T // 2, T // 2)
    all_of(recv_sem.at[1], hid_by_feature.at[pl.ds(0, 2 * (DV - 1))])

    def sum_block(b):
        total = jnp.zeros((F, TILE), F32)
        for q in range(TILE_ROW):
            k = b * TILE_ROW + q
            total = total + dot_nn(hid_by_feature[ids[0, k]], counts[k])
        agg_send[b] = total.astype(BF)

    def send_block(b):
        remote(agg_send.at[b], agg_recv.at[my_rows], send_sem.at[2], recv_sem.at[2], "dev", b)

    def aggregate(i, c):
        near = [i * 4 + u for u in range(4)]
        pairs = [
            (wrap(me + DV // 2 - m, DV), wrap(me + DV // 2 + 1 + m, DV)) for m in near
        ]
        for pair in pairs:
            for b in pair:
                sum_block(b)
        for low, high in pairs:
            send_block(low)
            pl.when(high != me)(lambda high=high: send_block(high))
        return c

    lax.fori_loop(0, DV // 8, aggregate, 0)
    agg_recv[my_rows, :] = agg_send[me]
    out_relay(*soon[3:])
    out_relay(*late)
    if HZ > 3:
        z_step(3)
    out_far()
    all_of(recv_sem.at[2], agg_recv.at[pl.ds(0, D - F)])

    agg_hidden = agg_recv[...].astype(F32).T.astype(BF)
    for j in range(HD // W):
        low = dot_nn(agg_hidden, w_out[:, :, :, j * W : (j + 1) * W].reshape(D, W))
        high = dot_nn(agg_hidden, w_out[:, :, :, HD + j * W : HD + (j + 1) * W].reshape(D, W))
        both = jnp.concatenate([low.reshape(R, TR, W), high.reshape(R, TR, W)], axis=1)
        both = both.astype(BF).reshape(Z, 2, 2 * TR, W)
        part_send[0, :, :, j * W : (j + 1) * W] = both[:, 0]
        part_send[1, :, :, j * W : (j + 1) * W] = both[:, 1]
    remote(part_send.at[1 - my_c], part_pair, send_sem.at[0], recv_sem.at[0], "rel", zc(0, 1))

    def wide(rows):
        return (jnp.concatenate([rows, rows], axis=0) if TR < 16 else rows).astype(BF)

    all_of(recv_sem.at[0], part_pair)
    part_sum[...] = (part_send[my_c].astype(F32) + part_pair[...].astype(F32)).astype(BF)
    for d in sorted(range(1, Z), key=lambda d: -min(d, Z - d)):
        remote(
            part_sum.at[lax.rem(my_z + d, Z)],
            part_recv.at[my_z],
            send_sem.at[3],
            recv_sem.at[3],
            "rel",
            zc(d),
        )
    part_recv[my_z] = part_sum[my_z]
    z_step(HZ)
    z_step(HZ + 1)
    og_rows = wide(og[...].astype(F32))
    grad_hidden_t = [dot_nt(og_rows, two[r]) for r in range(R)]
    all_of(recv_sem.at[3], part_recv.at[pl.ds(0, Z - 1)])
    total = part_recv[0].astype(F32)
    for z in range(1, Z):
        total = total + part_recv[z].astype(F32)
    agg = jnp.concatenate([total[:TR], total[TR:]], axis=1)
    gain_row = gain[...]
    inverse_norm = lax.rsqrt(jnp.mean(agg * agg, axis=1, keepdims=True) + eps_norm)
    normed = wide(agg * inverse_norm * gain_row)
    target_pre = [dot_nn(normed, twi[r]) for r in range(R)]
    grad_normed = jnp.zeros((normed.shape[0], D), F32)
    for r in range(R):
        grad_pre_t = (grad_hidden_t[r] * silu_slope(target_pre[r])).astype(BF)
        grad_normed = grad_normed + dot_nt(grad_pre_t, twi[r])
    scaled = grad_normed[:TR] * gain_row
    mean_term = jnp.mean(agg * scaled, axis=1, keepdims=True)
    ga_send[...] = folded(
        inverse_norm * (scaled - agg * inverse_norm * inverse_norm * mean_term)
    )
    for dz in sorted(range(1, Z), key=lambda d: -min(d, Z - d)):
        remote(ga_send, ga_recv.at[rd], send_sem.at[4], ga_sem.at[my_z], "rel", zc(dz))
    remote(ga_send, ga_recv.at[rd], send_sem.at[4], ga_pair_sem.at[0], "rel", zc(0, 1))
    ga_recv[rd] = ga_send[...]
    update = jnp.zeros((normed.shape[0], D), F32)
    for r in range(R):
        target_hidden = (target_pre[r] * jax.nn.sigmoid(target_pre[r])).astype(BF)
        update = update + dot_nn(target_hidden, two[r])
    upd_out[...] = (tfeat[...].astype(F32) + update[:TR]).astype(BF)
    put_upd = take(14, upd_out, upd_place)
    for dz in sorted(range(1, Z), key=lambda d: min(d, Z - d)):
        r = zc(dz)
        all_of(ga_sem.at[lax.div(r, 2)], ga_recv.at[r])
        remote(ga_recv.at[r], ga_recv.at[r], send_sem.at[4], ga_pair_sem.at[0], "rel", zc(0, 1))
    all_of(ga_pair_sem.at[0], ga_recv.at[pl.ds(0, Z)])

    held = ga_recv[...].astype(F32)
    held = jnp.concatenate([held[:, :TR, :], held[:, TR:, :]], axis=2)
    grad_agg = held.reshape(R * TR, D).astype(BF)
    blocks = W // F
    for j in range(D // W):
        value = dot_nt(grad_agg, w_out[j * blocks // X : (j + 1) * blocks // X].reshape(W, D))
        gt_send[j * W : (j + 1) * W, :] = value.T.astype(BF)
        if (j + 1) * W % HD == 0:
            half_done = (j + 1) * W // HD - 1
            over_half(half_done, 5, lambda part: gt_send.at[part], gt_recv.at[me])
    gt_recv[me] = gt_send[my_rows, :]
    runs[T] = jnp.zeros((F, TILE), F32)
    count_tiles(0, T, True)
    all_of(recv_sem.at[5], gt_recv.at[pl.ds(0, DV - 1)])

    def spread(i, running):
        for u in range(32):
            j = i * 32 + u
            term = dot_nn(gt_recv[tab[1, j]], counts[tab[0, j]])
            running = running * tab[2, j].astype(F32) + term
            runs[j] = running
        return running

    lax.fori_loop(0, T // 32, spread, jnp.zeros((F, TILE), F32))

    def settle(i, c):
        for u in range(8):
            b = i * 8 + u
            gh_send[b] = runs[tab[3, b]].astype(BF)
        return c

    lax.fori_loop(0, 2 * DV // 8, settle, 0)
    for h in range(2):
        over_dev(6 + h, lambda to: gh_send.at[2 * to + h], gh_recv.at[h, my_rows, :])
    gh_recv[:, my_rows, :] = gh_send[pl.ds(2 * me, 2)]

    for h in range(2):
        all_of(ring_send_sem.at[h], half[h].at[pl.ds(0, DV - 1)])
        all_of(z_send_sem.at[h], tgt[h].at[pl.ds(0, R - 1)])
    all_of(wout_send_sem.at[0], w_out.at[pl.ds(0, Y - 1), 0])
    all_of(wout_send_sem.at[1], w_out.at[:, pl.ds(0, 3)])
    all_of(send_sem.at[0], part_pair)
    all_of(send_sem.at[1], hid_by_feature.at[pl.ds(0, 2 * (DV - 1))])
    all_of(send_sem.at[2], agg_recv.at[pl.ds(0, D - F)])
    all_of(send_sem.at[3], part_recv.at[pl.ds(0, Z - 1)])
    all_of(send_sem.at[4], ga_recv.at[pl.ds(0, R - 1)])
    all_of(send_sem.at[5], gt_recv.at[pl.ds(0, DV - 1)])

    def put_grad(h, j):
        part = (pl.ds(h * TILE, TILE), pl.ds(pl.multiple_of(j * W, W), W))
        return pltpu.make_async_copy(
            grad_out.at[part], grad_place.at[part], copy_sem.at[15]
        )

    def slopes(j, c):
        cols = pl.ds(pl.multiple_of(j * W, W), W)
        pre[:, cols] = silu_slope(pre[:, cols])
        return c

    lax.fori_loop(0, D // W, slopes, 0)

    for h in range(2):
        these_rows = slice(h * TILE, (h + 1) * TILE)
        all_of(recv_sem.at[6 + h], gh_recv.at[h, pl.ds(0, D - F), :])

        def last_slope(j, c):
            cols = pl.ds(pl.multiple_of(j * W, W), W)
            value = gh_recv[h, cols, :].astype(F32).T * pre[these_rows, cols]
            grad_pre[these_rows, cols] = value.astype(BF)
            return c

        lax.fori_loop(0, D // W, last_slope, 0)

        def last_projection(j, c):
            cols = pl.ds(pl.multiple_of(j * W, W), W)
            these = pl.ds(j * blocks, blocks)
            value = dot_nt(grad_pre[these_rows, :HD], w_a[these].reshape(W, HD))
            value = value + dot_nt(grad_pre[these_rows, HD:], w_b[these].reshape(W, HD))
            grad_out[these_rows, cols] = value.astype(BF)
            put_grad(h, j).start()
            return c

        lax.fori_loop(0, D // W, last_projection, 0)
    put_upd.wait()
    all_of(copy_sem.at[15], grad_out)
    for h in range(2):
        all_of(send_sem.at[6 + h], gh_recv.at[h, pl.ds(0, D - F), :])


def shards(
    src_feat,
    rel_w_in,
    rel_w_out,
    tile_source,
    tile_edges,
    tile_count,
    target_feat,
    norm_gain,
    tgt_w_in,
    tgt_w_out,
    out_grad,
):
    DV = lax.axis_size("dev")
    R = lax.axis_size("rel")
    own_rows = src_feat[0]
    rows, D = own_rows.shape
    F = D // DV
    T = tile_source.shape[1]
    TR = target_feat.shape[0]
    X, Y, Z = RING_X, DV // RING_X, R // 2
    HT = tgt_w_in.shape[1]

    place = pl.BlockSpec(memory_space=pl.ANY)
    hbm = pl.BlockSpec(memory_space=pltpu.HBM)
    updated, grad_source = pl.pallas_call(
        functools.partial(whole_kernel, DV, R),
        out_shape=(
            pltpu.VMEM((TR, D), BF),
            pltpu.VMEM((rows, D), BF),
        ),
        in_specs=[hbm] * 11,
        out_specs=(place, place),
        scratch_shapes=[
            pltpu.SMEM((1, T), jnp.int32),
            pltpu.SMEM((1, T), jnp.int32),
            pltpu.VMEM((1, T), jnp.int32),
            pltpu.VMEM((4, T), jnp.int32),
            pltpu.SMEM((4, T), jnp.int32),
            pltpu.VMEM((TR, D), BF),
            pltpu.VMEM((1, D), F32),
            pltpu.VMEM((TR, D), BF),
            pltpu.VMEM((rows, D), BF),
            pltpu.VMEM((T, TILE), jnp.int32),
            pltpu.VMEM((DV, F, D // 2), BF),
            pltpu.VMEM((DV, F, D // 2), BF),
            pltpu.VMEM((Y, X, F, D), BF),
            pltpu.VMEM((R, D, HT), BF),
            pltpu.VMEM((R, HT, D), BF),
            pltpu.VMEM((rows, D), F32),
            pltpu.VMEM((2, D, TILE), BF),
            pltpu.VMEM((2 * DV, F, TILE), BF),
            pltpu.VMEM((T, TILE, TILE), BF),
            pltpu.VMEM((DV, F, TILE), BF),
            pltpu.VMEM((D, TILE), BF),
            pltpu.VMEM((2, Z, 2 * TR, D // 2), BF),
            pltpu.VMEM((Z, 2 * TR, D // 2), BF),
            pltpu.VMEM((Z, 2 * TR, D // 2), BF),
            pltpu.VMEM((Z, 2 * TR, D // 2), BF),
            pltpu.VMEM((2 * TR, D // 2), BF),
            pltpu.VMEM((R, 2 * TR, D // 2), BF),
            pltpu.VMEM((D, TILE), BF),
            pltpu.VMEM((DV, F, TILE), BF),
            pltpu.VMEM((T + 1, F, TILE), F32),
            pltpu.VMEM((2 * DV, F, TILE), BF),
            pltpu.VMEM((2, D, TILE), BF),
            pltpu.VMEM((rows, D), BF),
            pltpu.VMEM((TR, D), BF),
            pltpu.VMEM((rows, D), BF),
            pltpu.SemaphoreType.DMA((16,)),
            pltpu.SemaphoreType.DMA((2, DV)),
            pltpu.SemaphoreType.DMA((2,)),
            pltpu.SemaphoreType.DMA((Y,)),
            pltpu.SemaphoreType.DMA((2, Y)),
            pltpu.SemaphoreType.DMA((1,)),
            pltpu.SemaphoreType.DMA((2,)),
            pltpu.SemaphoreType.DMA((2, Z)),
            pltpu.SemaphoreType.DMA((2,)),
            pltpu.SemaphoreType.DMA((2,)),
            pltpu.SemaphoreType.DMA((Z,)),
            pltpu.SemaphoreType.DMA((1,)),
            pltpu.SemaphoreType.DMA((8,)),
            pltpu.SemaphoreType.DMA((8,)),
        ],
        compiler_params=pltpu.CompilerParams(
            collective_id=0, has_side_effects=True, vmem_limit_bytes=60 * 1024 * 1024
        ),
        name="whole_layer",
    )(
        tile_source,
        tile_count,
        own_rows,
        rel_w_in[0],
        rel_w_out[0],
        tile_edges[0],
        target_feat,
        norm_gain[None, :],
        tgt_w_in,
        tgt_w_out,
        out_grad,
    )
    return (updated, grad_source[None])


def solution(mesh):
    placed = (
        P("rel", "dev", None),
        P("rel", "dev", None),
        P("rel", "dev", None),
        P("rel", None),
        P("rel", None, None),
        P("rel", None),
        P(("dev", "rel"), None),
        P(),
        P(None, "rel"),
        P("rel", None),
        P(("dev", "rel"), None),
    )
    return jax.shard_map(
        shards,
        mesh=mesh,
        in_specs=placed,
        out_specs=(P(("dev", "rel"), None), P("rel", "dev", None)),
        check_vma=False,
    )
```

```python
import functools

import jax
import jax.numpy as jnp
from jax import lax
from jax.experimental import pallas as pl
from jax.experimental.pallas import tpu as pltpu
from jax.sharding import PartitionSpec as P

TILE = 128
TILE_ROW = 4
RING_X = 4

eps_norm = 1e-06

BF = jnp.bfloat16
F32 = jnp.float32
MESH = pl.DeviceIdType.MESH


def silu_slope(values):
    sigma = jax.nn.sigmoid(values)
    return sigma * (1.0 + values * (1.0 - sigma))


def dot_nn(a, b):
    return lax.dot_general(a, b, (((1,), (0,)), ((), ())), preferred_element_type=F32)


def dot_nt(a, b):
    return lax.dot_general(a, b, (((1,), (1,)), ((), ())), preferred_element_type=F32)


def whole_kernel(
    DV,
    R,
    ids_in,
    live_in,
    src_in,
    win_in,
    wout_in,
    edges_in,
    tfeat_in,
    gain_in,
    twi_in,
    two_in,
    og_in,
    upd_place,
    grad_place,
    ids,
    live,
    ids_v,
    tab_v,
    tab,
    tfeat,
    gain,
    og,
    src,
    edges,
    w_a,
    w_b,
    w_out,
    twi,
    two,
    pre,
    hid_t,
    hid_by_feature,
    counts,
    agg_send,
    agg_recv,
    part_send,
    part_pair,
    part_sum,
    part_recv,
    ga_send,
    ga_recv,
    gt_send,
    gt_recv,
    runs,
    gh_send,
    gh_recv,
    grad_pre,
    upd_out,
    grad_out,
    copy_sem,
    ring_sem,
    ring_send_sem,
    y_sem,
    x_sem,
    far_sem,
    wout_send_sem,
    z_sem,
    z_pair_sem,
    z_send_sem,
    ga_sem,
    ga_pair_sem,
    send_sem,
    recv_sem,
):
    D = src.shape[1]
    HD = D // 2
    F = D // DV
    T = ids.shape[1]
    TR = tfeat.shape[0]
    X = RING_X
    Y = DV // X
    HY = Y // 2
    Z = R // 2
    HZ = Z // 2
    W = min(256, HD)
    rd = lax.axis_index("rel")
    me = lax.axis_index("dev")
    my_y = me // X
    my_x = lax.rem(me, X)
    my_z = rd // 2
    my_c = lax.rem(rd, 2)

    def col(dx):
        return lax.rem(my_x + dx + X, X)

    def row(dy):
        return lax.rem(my_y + dy + Y, Y)

    def at(dy, dx):
        return row(dy) * X + col(dx)

    def zc(dz, dc=0):
        return lax.rem(my_z + dz + Z, Z) * 2 + lax.rem(my_c + dc, 2)

    barrier = pltpu.get_barrier_semaphore()

    near_dev = (at(1, 0), at(-1, 0), at(0, 1), at(0, -1), at(0, 2))
    near_rel = (zc(1), zc(-1), zc(0, 1))
    for to in near_dev:
        pl.semaphore_signal(barrier, inc=1, device_id={"dev": to}, device_id_type=MESH)
    for to in near_rel:
        pl.semaphore_signal(barrier, inc=1, device_id={"rel": to}, device_id_type=MESH)
    def take(n, source, place):
        copy = pltpu.make_async_copy(source, place, copy_sem.at[n])
        copy.start()
        return copy

    own_a = take(0, win_in.at[:, pl.ds(0, HD)], w_a.at[me])
    own_b = take(1, win_in.at[:, pl.ds(HD, HD)], w_b.at[me])
    own_twi = take(2, twi_in, twi.at[rd])
    own_two = take(3, two_in, two.at[rd])
    own_out = take(4, wout_in, w_out.at[my_y, my_x])
    own_ids = take(7, ids_in, ids_v)
    own_src = take(5, src_in, src)
    own_edges = take(6, edges_in, edges)
    own_small = [
        take(8, ids_in, ids),
        take(9, live_in, live),
        take(10, tfeat_in, tfeat),
        take(11, gain_in, gain),
        take(12, og_in, og),
    ]

    own_a.wait()
    own_b.wait()
    pl.semaphore_wait(barrier, len(near_dev) + len(near_rel))

    def remote(piece, place, sent, got, axis, to):
        pltpu.make_async_remote_copy(
            src_ref=piece,
            dst_ref=place,
            send_sem=sent,
            recv_sem=got,
            device_id={axis: to},
            device_id_type=MESH,
        ).start()

    def all_of(sem, view):
        pltpu.make_async_copy(view, view, sem).wait()

    half = (w_a, w_b)

    def push(h, block, to):
        piece = half[h].at[block]
        remote(piece, piece, ring_send_sem.at[h], ring_sem.at[h, block], "dev", to)

    def arrive(h, block):
        all_of(ring_sem.at[h, block], half[h].at[block])

    def begin_in():
        push(0, me, at(1, 0))
        push(0, me, at(-1, 0))
        push(0, me, at(0, 1))
        push(0, me, at(0, -1))
        push(1, me, at(1, 0))
        push(1, me, at(-1, 0))
        push(0, me, at(0, 2))
        push(1, me, at(0, 1))
        push(1, me, at(0, -1))

    def relay_x(dy):
        even = lax.rem(row(dy), 2) == 0
        arrive(1, at(dy, -1))
        arrive(1, at(dy, 1))
        push(
            1,
            jnp.where(even, at(dy, -1), at(dy, 1)),
            jnp.where(even, at(0, 1), at(0, -1)),
        )

    def first_half(s):
        def column(i, c):
            dx = jnp.where(i == 3, 2, jnp.where(i == 2, 3, i))
            if s == 0:
                arrive(0, at(0, dx))
                push(0, at(0, dx), at(1, 0))
                push(0, at(0, dx), at(-1, 0))
            elif s < HY:
                arrive(0, at(-s, dx))
                if s < HY - 1:
                    push(0, at(-s, dx), at(1, 0))
                arrive(0, at(s, dx))
                if s < HY - 1:
                    push(0, at(s, dx), at(-1, 0))
                else:
                    even = lax.rem(my_x + dx, 2) == 0
                    push(
                        0,
                        jnp.where(even, at(-s, dx), at(s, dx)),
                        jnp.where(even, at(1, 0), at(-1, 0)),
                    )
            else:
                arrive(0, at(HY, dx))
            return c

        lax.fori_loop(1 if s == 0 else 0, X, column, 0)

    def to_row(dy, far):
        push(1, at(dy, 0), at(0, 1))
        push(1, at(dy, 0), at(0, -1))
        if far:
            push(1, at(dy, 0), at(0, 2))

    def second_half(s):
        far = s >= HY - 1
        if 1 <= s < HY:
            for d in (-s, s):
                arrive(1, at(d, 0))
                if s < HY - 1:
                    push(1, at(d, 0), at(1 if d < 0 else -1, 0))
            if s == HY - 1:
                even = lax.rem(my_x, 2) == 0
                push(
                    1,
                    jnp.where(even, at(-s, 0), at(s, 0)),
                    jnp.where(even, at(1, 0), at(-1, 0)),
                )
            for d in (-s, s):
                to_row(d, far)
        elif s == HY:
            arrive(1, at(HY, 0))
            to_row(HY, far)
        if s == 1:
            relay_x(0)
        elif 2 <= s < HY:
            relay_x(-(s - 1))
            relay_x(s - 1)

    def second_rest():
        for d in (-(HY - 1), HY - 1, HY):
            arrive(1, at(d, 1))
            arrive(1, at(d, -1))
        if HY == 2:
            pass

        def rest(i, c):
            arrive(1, i * X + col(2))
            return c

        lax.fori_loop(0, Y, rest, 0)

    def out_push(y, to):
        piece = w_out.at[y, my_x]
        remote(piece, piece, wout_send_sem.at[0], y_sem.at[y], "dev", to)

    def out_arrive(y):
        all_of(y_sem.at[y], w_out.at[y, my_x])

    def out_y(s):
        if s == 0:
            out_push(my_y, at(1, 0))
            out_push(my_y, at(-1, 0))
        elif s < HY:
            out_arrive(row(-s))
            if s < HY - 1:
                out_push(row(-s), at(1, 0))
            out_arrive(row(s))
            if s < HY - 1:
                out_push(row(s), at(-1, 0))
            else:
                even = lax.rem(my_x, 2) == 0
                out_push(
                    jnp.where(even, row(-s), row(s)), jnp.where(even, at(1, 0), at(-1, 0))
                )
        else:
            out_arrive(row(HY))

    def out_x(*rows):
        for dy in rows:
            piece = w_out.at[row(dy), my_x]
            for side in (0, 1):
                to = at(0, 1) if side == 0 else at(0, -1)
                remote(piece, piece, wout_send_sem.at[1], x_sem.at[side, row(dy)], "dev", to)

    def out_relay(*rows):
        for dy in rows:
            y = row(dy)
            even = lax.rem(y, 2) == 0
            all_of(x_sem.at[0, y], w_out.at[y, col(-1)])
            all_of(x_sem.at[1, y], w_out.at[y, col(1)])
            piece = w_out.at[y, jnp.where(even, col(-1), col(1))]
            to = jnp.where(even, at(0, 1), at(0, -1))
            remote(piece, piece, wout_send_sem.at[1], far_sem.at[0], "dev", to)

    def out_far():
        all_of(far_sem.at[0], w_out.at[:, col(2)])

    tgt = (twi, two)

    def z_push(w, r, to):
        piece = tgt[w].at[r]
        remote(piece, piece, z_send_sem.at[w], z_sem.at[w, lax.div(r, 2)], "rel", to)

    def z_pair(w, r):
        piece = tgt[w].at[r]
        remote(piece, piece, z_send_sem.at[w], z_pair_sem.at[w], "rel", zc(0, 1))

    def z_arrive(w, r):
        all_of(z_sem.at[w, lax.div(r, 2)], tgt[w].at[r])

    def z_step(s, weights=(0, 1)):
        for w in weights:
            if s == 0:
                z_push(w, rd, zc(1))
                z_push(w, rd, zc(-1))
                z_pair(w, rd)
            elif s < HZ:
                z_arrive(w, zc(-s))
                if s < HZ - 1 or w == 0:
                    z_push(w, zc(-s), zc(1))
                z_arrive(w, zc(s))
                if s < HZ - 1 or w == 1:
                    z_push(w, zc(s), zc(-1))
                z_pair(w, zc(-s))
                z_pair(w, zc(s))
            elif s == HZ:
                z_arrive(w, zc(HZ))
                z_pair(w, zc(HZ))
            else:
                all_of(z_pair_sem.at[w], tgt[w].at[pl.ds(0, Z)])

    def wrap(i, n):
        return i - jnp.where(i >= n, n, 0)

    def over_dev(n, piece, place):
        def send(to):
            to = wrap(to, DV)
            remote(piece(to), place, send_sem.at[n], recv_sem.at[n], "dev", to)

        send(me + DV // 2)

        def pair(m, c):
            send(me + DV // 2 - m)
            send(me + DV // 2 + m)
            return c

        lax.fori_loop(1, DV // 2, pair, 0)

    def folded(rows):
        return jnp.concatenate([rows[..., :HD], rows[..., HD:]], axis=-2).astype(BF)

    def count_tiles(first, number, turned=False):
        lattice = lax.broadcasted_iota(jnp.int32, (TILE, TILE), 0).astype(F32).astype(BF)
        slots = lax.broadcasted_iota(jnp.int32, (1, TILE), 1)
        one = jnp.ones((TILE, TILE), BF)
        none = jnp.zeros((TILE, TILE), BF)

        def hot(spots):
            rows = jnp.broadcast_to(spots.astype(F32), (16, TILE)).astype(BF)
            return jnp.where(lattice == jnp.concatenate([rows] * (TILE // 16), axis=0), one, none)

        def some(i, c):
            for u in range(8):
                k = first + i * 8 + u
                codes = edges[pl.ds(k, 1), :]
                s_at = jnp.bitwise_and(codes, TILE - 1)
                t_at = jnp.where(slots < live[0, k], jnp.right_shift(codes, 7), -1)
                s_hot, t_hot = hot(s_at), hot(t_at)
                pair = (t_hot, s_hot) if turned else (s_hot, t_hot)
                counts[k] = dot_nt(*pair).astype(BF)
            return c

        lax.fori_loop(0, number // 8, some, 0)

    def slice_of(p):
        x = lax.rem(p, X)
        return (x // 2) * (DV // 2) + (p // X) * 2 + lax.rem(x, 2)

    mine = slice_of(me)
    my_rows = pl.ds(pl.multiple_of(mine * F, F), F)

    def over_half(h, n, piece, place):
        def send(y, near=False):
            y = wrap(y, Y)
            for bit in range(2):
                to = y * X + 2 * h + bit

                def one(to=to, bit=bit):
                    part = pl.ds(pl.multiple_of((h * (DV // 2) + y * 2 + bit) * F, F), F)
                    remote(piece(part), place, send_sem.at[n], recv_sem.at[n], "dev", to)

                if near:
                    pl.when(to != me)(one)
                else:
                    one()

        send(my_y + HY)

        def pair(m, c):
            send(my_y + HY - m)
            send(my_y + HY + m)
            return c

        lax.fori_loop(1, HY, pair, 0)
        send(my_y, True)

    def first_projection(h):
        def some(j, c):
            cols = pl.ds(pl.multiple_of(j * W, W), W)
            value = dot_nn(src[...], half[h][:, :, cols].reshape(D, W))
            there = pl.ds(pl.multiple_of(h * HD + j * W, W), W)
            pre[:, there] = value
            turned = (value * jax.nn.sigmoid(value)).T.astype(BF)
            hid_t[0, there, :] = turned[:, :TILE]
            hid_t[1, there, :] = turned[:, TILE:]
            return c

        lax.fori_loop(0, HD // W, some, 0)

        over_half(
            h, 1, lambda part: hid_t.at[:, part, :], hid_by_feature.at[pl.ds(2 * me, 2)]
        )

    def make_tables():
        spread_ids = jnp.broadcast_to(ids_v[...], (T, T))
        down = spread_ids.T
        ii = lax.broadcasted_iota(jnp.int32, (T, T), 0)
        jj = lax.broadcasted_iota(jnp.int32, (T, T), 1)

        def over_tiles(mask, value):
            return jnp.sum(jnp.where(mask, value, 0), axis=0, keepdims=True)

        earlier = (down < spread_ids) | ((down == spread_ids) & (ii < jj))
        rank = jnp.broadcast_to(over_tiles(earlier, 1), (T, T)).T
        order = over_tiles(rank == jj, ii)
        here = over_tiles(rank == jj, down)
        before = over_tiles(rank + 1 == jj, down + 1) - 1
        upto = over_tiles(down <= jj, 1)
        named = over_tiles(down == jj, 1)
        tab_v[0:1, :] = order
        tab_v[1:2, :] = jnp.right_shift(order, 2)
        tab_v[2:3, :] = jnp.where(here == before, 1, 0)
        tab_v[3:4, :] = jnp.where(named > 0, upto - 1, T)

    begin_in()
    own_twi.wait()
    own_two.wait()
    z_step(0)
    own_ids.wait()
    make_tables()
    own_tab = take(13, tab_v, tab)
    own_out.wait()
    soon = [d for n in range(HY - 1) for d in ((-n, n) if n else (0,))]
    late = [-(HY - 1), HY - 1, HY]
    for s in range(HY + 1):
        first_half(s)
        second_half(s)
        if s == 0:
            out_x(0)
        if s == HY - 3:
            out_y(0)
        if s == HY - 2:
            z_step(1, (0,))
        if s == HY - 1:
            z_step(1, (1,))
            out_y(1)
            out_x(*soon[1:3])
    for s in range(2, HY - 1):
        out_y(s)
    own_src.wait()
    first_projection(0)
    own_edges.wait()
    for copy in own_small:
        copy.wait()
    own_tab.wait()
    count_tiles(0, T // 2)
    out_y(HY - 1)
    second_rest()
    first_projection(1)
    hid_by_feature[pl.ds(2 * me, 2)] = hid_t[:, my_rows, :]
    out_x(*soon[3:])
    out_x(-(HY - 1), HY - 1)
    if HZ > 2:
        z_step(2, (0,))
    out_y(HY)
    out_x(HY)
    out_relay(*soon[:3])
    if HZ > 2:
        z_step(2, (1,))
    count_tiles(T // 2, T // 2)
    all_of(recv_sem.at[1], hid_by_feature.at[pl.ds(0, 2 * (DV - 1))])

    def sum_block(b):
        total = jnp.zeros((F, TILE), F32)
        for q in range(TILE_ROW):
            k = b * TILE_ROW + q
            total = total + dot_nn(hid_by_feature[ids[0, k]], counts[k])
        agg_send[b] = total.astype(BF)

    def send_block(b):
        remote(agg_send.at[b], agg_recv.at[my_rows], send_sem.at[2], recv_sem.at[2], "dev", b)

    def aggregate(i, c):
        near = [i * 4 + u for u in range(4)]
        pairs = [
            (wrap(me + DV // 2 - m, DV), wrap(me + DV // 2 + 1 + m, DV)) for m in near
        ]
        for pair in pairs:
            for b in pair:
                sum_block(b)
        for low, high in pairs:
            send_block(low)
            pl.when(high != me)(lambda high=high: send_block(high))
        return c

    lax.fori_loop(0, DV // 8, aggregate, 0)
    agg_recv[my_rows, :] = agg_send[me]
    out_relay(*soon[3:])
    out_relay(*late)
    if HZ > 3:
        z_step(3)
    out_far()
    all_of(recv_sem.at[2], agg_recv.at[pl.ds(0, D - F)])

    agg_hidden = agg_recv[...].astype(F32).T.astype(BF)
    for j in range(HD // W):
        low = dot_nn(agg_hidden, w_out[:, :, :, j * W : (j + 1) * W].reshape(D, W))
        high = dot_nn(agg_hidden, w_out[:, :, :, HD + j * W : HD + (j + 1) * W].reshape(D, W))
        both = jnp.concatenate([low.reshape(R, TR, W), high.reshape(R, TR, W)], axis=1)
        both = both.astype(BF).reshape(Z, 2, 2 * TR, W)
        part_send[0, :, :, j * W : (j + 1) * W] = both[:, 0]
        part_send[1, :, :, j * W : (j + 1) * W] = both[:, 1]
    remote(part_send.at[1 - my_c], part_pair, send_sem.at[0], recv_sem.at[0], "rel", zc(0, 1))

    def wide(rows):
        return (jnp.concatenate([rows, rows], axis=0) if TR < 16 else rows).astype(BF)

    all_of(recv_sem.at[0], part_pair)
    part_sum[...] = (part_send[my_c].astype(F32) + part_pair[...].astype(F32)).astype(BF)
    for d in sorted(range(1, Z), key=lambda d: -min(d, Z - d)):
        remote(
            part_sum.at[lax.rem(my_z + d, Z)],
            part_recv.at[my_z],
            send_sem.at[3],
            recv_sem.at[3],
            "rel",
            zc(d),
        )
    part_recv[my_z] = part_sum[my_z]
    z_step(HZ)
    z_step(HZ + 1)
    og_rows = wide(og[...].astype(F32))
    grad_hidden_t = [dot_nt(og_rows, two[r]) for r in range(R)]
    all_of(recv_sem.at[3], part_recv.at[pl.ds(0, Z - 1)])
    total = part_recv[0].astype(F32)
    for z in range(1, Z):
        total = total + part_recv[z].astype(F32)
    agg = jnp.concatenate([total[:TR], total[TR:]], axis=1)
    gain_row = gain[...]
    inverse_norm = lax.rsqrt(jnp.mean(agg * agg, axis=1, keepdims=True) + eps_norm)
    normed = wide(agg * inverse_norm * gain_row)
    target_pre = [dot_nn(normed, twi[r]) for r in range(R)]
    grad_normed = jnp.zeros((normed.shape[0], D), F32)
    for r in range(R):
        grad_pre_t = (grad_hidden_t[r] * silu_slope(target_pre[r])).astype(BF)
        grad_normed = grad_normed + dot_nt(grad_pre_t, twi[r])
    scaled = grad_normed[:TR] * gain_row
    mean_term = jnp.mean(agg * scaled, axis=1, keepdims=True)
    ga_send[...] = folded(
        inverse_norm * (scaled - agg * inverse_norm * inverse_norm * mean_term)
    )
    for dz in sorted(range(1, Z), key=lambda d: -min(d, Z - d)):
        remote(ga_send, ga_recv.at[rd], send_sem.at[4], ga_sem.at[my_z], "rel", zc(dz))
    remote(ga_send, ga_recv.at[rd], send_sem.at[4], ga_pair_sem.at[0], "rel", zc(0, 1))
    ga_recv[rd] = ga_send[...]
    update = jnp.zeros((normed.shape[0], D), F32)
    for r in range(R):
        target_hidden = (target_pre[r] * jax.nn.sigmoid(target_pre[r])).astype(BF)
        update = update + dot_nn(target_hidden, two[r])
    upd_out[...] = (tfeat[...].astype(F32) + update[:TR]).astype(BF)
    put_upd = take(14, upd_out, upd_place)
    for dz in sorted(range(1, Z), key=lambda d: min(d, Z - d)):
        r = zc(dz)
        all_of(ga_sem.at[lax.div(r, 2)], ga_recv.at[r])
        remote(ga_recv.at[r], ga_recv.at[r], send_sem.at[4], ga_pair_sem.at[0], "rel", zc(0, 1))
    all_of(ga_pair_sem.at[0], ga_recv.at[pl.ds(0, Z)])

    held = ga_recv[...].astype(F32)
    held = jnp.concatenate([held[:, :TR, :], held[:, TR:, :]], axis=2)
    grad_agg = held.reshape(R * TR, D).astype(BF)
    blocks = W // F
    for j in range(D // W):
        value = dot_nt(grad_agg, w_out[j * blocks // X : (j + 1) * blocks // X].reshape(W, D))
        gt_send[j * W : (j + 1) * W, :] = value.T.astype(BF)
        if (j + 1) * W % HD == 0:
            half_done = (j + 1) * W // HD - 1
            over_half(half_done, 5, lambda part: gt_send.at[part], gt_recv.at[me])
    gt_recv[me] = gt_send[my_rows, :]
    runs[T] = jnp.zeros((F, TILE), F32)
    count_tiles(0, T, True)
    all_of(recv_sem.at[5], gt_recv.at[pl.ds(0, DV - 1)])

    def spread(i, running):
        for u in range(32):
            j = i * 32 + u
            term = dot_nn(gt_recv[tab[1, j]], counts[tab[0, j]])
            running = running * tab[2, j].astype(F32) + term
            runs[j] = running
        return running

    lax.fori_loop(0, T // 32, spread, jnp.zeros((F, TILE), F32))

    def settle(i, c):
        for u in range(8):
            b = i * 8 + u
            gh_send[b] = runs[tab[3, b]].astype(BF)
        return c

    lax.fori_loop(0, 2 * DV // 8, settle, 0)
    over_dev(6, lambda to: gh_send.at[pl.ds(2 * to, 2)], gh_recv.at[:, my_rows, :])
    gh_recv[:, my_rows, :] = gh_send[pl.ds(2 * me, 2)]

    for h in range(2):
        all_of(ring_send_sem.at[h], half[h].at[pl.ds(0, DV - 1)])
        all_of(z_send_sem.at[h], tgt[h].at[pl.ds(0, R - 1)])
    all_of(wout_send_sem.at[0], w_out.at[pl.ds(0, Y - 1), 0])
    all_of(wout_send_sem.at[1], w_out.at[:, pl.ds(0, 3)])
    all_of(send_sem.at[0], part_pair)
    all_of(send_sem.at[1], hid_by_feature.at[pl.ds(0, 2 * (DV - 1))])
    all_of(send_sem.at[2], agg_recv.at[pl.ds(0, D - F)])
    all_of(send_sem.at[3], part_recv.at[pl.ds(0, Z - 1)])
    all_of(send_sem.at[4], ga_recv.at[pl.ds(0, R - 1)])
    all_of(send_sem.at[5], gt_recv.at[pl.ds(0, DV - 1)])

    def put_grad(h, j):
        part = (pl.ds(h * TILE, TILE), pl.ds(pl.multiple_of(j * W, W), W))
        return pltpu.make_async_copy(
            grad_out.at[part], grad_place.at[part], copy_sem.at[15]
        )

    def slopes(j, c):
        cols = pl.ds(pl.multiple_of(j * W, W), W)
        pre[:, cols] = silu_slope(pre[:, cols])
        return c

    lax.fori_loop(0, D // W, slopes, 0)

    all_of(recv_sem.at[6], gh_recv.at[:, pl.ds(0, D - F), :])
    for h in range(2):
        these_rows = slice(h * TILE, (h + 1) * TILE)

        def last_slope(j, c):
            cols = pl.ds(pl.multiple_of(j * W, W), W)
            value = gh_recv[h, cols, :].astype(F32).T * pre[these_rows, cols]
            grad_pre[these_rows, cols] = value.astype(BF)
            return c

        lax.fori_loop(0, D // W, last_slope, 0)

        def last_projection(j, c):
            cols = pl.ds(pl.multiple_of(j * W, W), W)
            these = pl.ds(j * blocks, blocks)
            value = dot_nt(grad_pre[these_rows, :HD], w_a[these].reshape(W, HD))
            value = value + dot_nt(grad_pre[these_rows, HD:], w_b[these].reshape(W, HD))
            grad_out[these_rows, cols] = value.astype(BF)
            put_grad(h, j).start()
            return c

        lax.fori_loop(0, D // W, last_projection, 0)
    put_upd.wait()
    all_of(copy_sem.at[15], grad_out)
    all_of(send_sem.at[6], gh_recv.at[:, pl.ds(0, D - F), :])


def shards(
    src_feat,
    rel_w_in,
    rel_w_out,
    tile_source,
    tile_edges,
    tile_count,
    target_feat,
    norm_gain,
    tgt_w_in,
    tgt_w_out,
    out_grad,
):
    DV = lax.axis_size("dev")
    R = lax.axis_size("rel")
    own_rows = src_feat[0]
    rows, D = own_rows.shape
    F = D // DV
    T = tile_source.shape[1]
    TR = target_feat.shape[0]
    X, Y, Z = RING_X, DV // RING_X, R // 2
    HT = tgt_w_in.shape[1]

    place = pl.BlockSpec(memory_space=pl.ANY)
    hbm = pl.BlockSpec(memory_space=pltpu.HBM)
    updated, grad_source = pl.pallas_call(
        functools.partial(whole_kernel, DV, R),
        out_shape=(
            pltpu.VMEM((TR, D), BF),
            pltpu.VMEM((rows, D), BF),
        ),
        in_specs=[hbm] * 11,
        out_specs=(place, place),
        scratch_shapes=[
            pltpu.SMEM((1, T), jnp.int32),
            pltpu.SMEM((1, T), jnp.int32),
            pltpu.VMEM((1, T), jnp.int32),
            pltpu.VMEM((4, T), jnp.int32),
            pltpu.SMEM((4, T), jnp.int32),
            pltpu.VMEM((TR, D), BF),
            pltpu.VMEM((1, D), F32),
            pltpu.VMEM((TR, D), BF),
            pltpu.VMEM((rows, D), BF),
            pltpu.VMEM((T, TILE), jnp.int32),
            pltpu.VMEM((DV, F, D // 2), BF),
            pltpu.VMEM((DV, F, D // 2), BF),
            pltpu.VMEM((Y, X, F, D), BF),
            pltpu.VMEM((R, D, HT), BF),
            pltpu.VMEM((R, HT, D), BF),
            pltpu.VMEM((rows, D), F32),
            pltpu.VMEM((2, D, TILE), BF),
            pltpu.VMEM((2 * DV, F, TILE), BF),
            pltpu.VMEM((T, TILE, TILE), BF),
            pltpu.VMEM((DV, F, TILE), BF),
            pltpu.VMEM((D, TILE), BF),
            pltpu.VMEM((2, Z, 2 * TR, D // 2), BF),
            pltpu.VMEM((Z, 2 * TR, D // 2), BF),
            pltpu.VMEM((Z, 2 * TR, D // 2), BF),
            pltpu.VMEM((Z, 2 * TR, D // 2), BF),
            pltpu.VMEM((2 * TR, D // 2), BF),
            pltpu.VMEM((R, 2 * TR, D // 2), BF),
            pltpu.VMEM((D, TILE), BF),
            pltpu.VMEM((DV, F, TILE), BF),
            pltpu.VMEM((T + 1, F, TILE), F32),
            pltpu.VMEM((2 * DV, F, TILE), BF),
            pltpu.VMEM((2, D, TILE), BF),
            pltpu.VMEM((rows, D), BF),
            pltpu.VMEM((TR, D), BF),
            pltpu.VMEM((rows, D), BF),
            pltpu.SemaphoreType.DMA((16,)),
            pltpu.SemaphoreType.DMA((2, DV)),
            pltpu.SemaphoreType.DMA((2,)),
            pltpu.SemaphoreType.DMA((Y,)),
            pltpu.SemaphoreType.DMA((2, Y)),
            pltpu.SemaphoreType.DMA((1,)),
            pltpu.SemaphoreType.DMA((2,)),
            pltpu.SemaphoreType.DMA((2, Z)),
            pltpu.SemaphoreType.DMA((2,)),
            pltpu.SemaphoreType.DMA((2,)),
            pltpu.SemaphoreType.DMA((Z,)),
            pltpu.SemaphoreType.DMA((1,)),
            pltpu.SemaphoreType.DMA((7,)),
            pltpu.SemaphoreType.DMA((7,)),
        ],
        compiler_params=pltpu.CompilerParams(
            collective_id=0, has_side_effects=True, vmem_limit_bytes=60 * 1024 * 1024
        ),
        name="whole_layer",
    )(
        tile_source,
        tile_count,
        own_rows,
        rel_w_in[0],
        rel_w_out[0],
        tile_edges[0],
        target_feat,
        norm_gain[None, :],
        tgt_w_in,
        tgt_w_out,
        out_grad,
    )
    return (updated, grad_source[None])


def solution(mesh):
    placed = (
        P("rel", "dev", None),
        P("rel", "dev", None),
        P("rel", "dev", None),
        P("rel", None),
        P("rel", None, None),
        P("rel", None),
        P(("dev", "rel"), None),
        P(),
        P(None, "rel"),
        P("rel", None),
        P(("dev", "rel"), None),
    )
    return jax.shard_map(
        shards,
        mesh=mesh,
        in_specs=placed,
        out_specs=(P(("dev", "rel"), None), P("rel", "dev", None)),
        check_vma=False,
    )
```
